512 devices in a mesh: dp: 128 (over x, z, core), mp: 4 (over y).
Axes of the slice: x: 4, y: 4, z: 16, core: 2. Of those that a mesh axis runs over, the one named last changes fastest.
Arguments:
- x_in: bfloat16 [16384, 1024], P('dp', 'mp'), may hold values from -90 to 90
- gain: float32 [1024], replicated, may hold values from 0.25 to 1.75
- w_in: bfloat16 [1024, 4096], P('mp'), may hold values from -0.5 to 0.5
- w_out: bfloat16 [1024, 4096], P('mp'), may hold values from -0.1875 to 0.1875
- grad_out: bfloat16 [16384, 1024], P('dp', 'mp'), may hold values from -6 to 6
- block_cols: int32 [4, 256], P('mp'), may hold values from 0 to 127, as said below
- slots: int32 [4, 256], P('mp'), may hold values from 0 to 511, as said below
Outputs:
- branch: bfloat16 [16384, 1024], P('dp', 'mp')
- grad_normed: bfloat16 [16384, 1024], P('dp', 'mp')
- owned_grad: float32 [4, 512, 4096], P('mp', 'dp')
The draws below stay inside these ranges and needn't reach their ends.
Inputs may be any that keep to these rules, and one draw needn't show every extreme that they name: Within one row of block_cols, the 16 entries k with the same k // 16 are distinct. The entries of one row of slots are distinct; slot s lies on index s // 4 of dp. In each row every index of dp holds at most 4 slots that are named, and some index holds exactly 4.
All inputs are finite; a program needn't handle non-finite values.
Results may differ from the reference program's by a relative error of at most 0.0062.
Values may be sent and summed in bfloat16 or wider, within the bound.
A program may use at most 128 MiB of HBM per device.

```python
import math
import jax
import jax.numpy as jnp
from jax import lax

D = 1024
FF = 32768
BLK = 64
DENS = 8
TOK_DEV = 128
TOKENS = 16384
NRB = 16
NCB = 128
KB = 256
KR = 16
CAP = 4
N_DP = 128
N_MP = 4


def draw_x_in(key, part):
    key_base, key_cols, key_rows = jax.random.split(key, 3)
    column = jnp.arange(D, dtype=jnp.float32)
    rising = 1.0 + 2.0 * column / (D - 1)
    base = jax.random.truncated_normal(key_base, -4.0, 4.0, (TOKENS, D), jnp.float32)
    col_scale = jnp.exp(jax.random.uniform(key_cols, (1, D), jnp.float32, -1.2, 1.2))
    row_scale = jnp.exp(jax.random.uniform(key_rows, (TOKENS, 1), jnp.float32, -0.7, 0.7))
    return (base * col_scale * rising * row_scale).astype(jnp.bfloat16)


def draw_block_cols(key, part):

    def one_shard(shard_key):
        key_hot, key_score = jax.random.split(shard_key)
        hot = (jax.random.permutation(key_hot, NCB) < NCB // 8).astype(jnp.int32)
        scores = jax.random.randint(key_score, (NRB, NCB), 0, 65536) + hot[None, :] * 32768
        scores = scores * NCB + jnp.arange(NCB, dtype=jnp.int32)[None, :]
        chosen = lax.top_k(scores, KR)[1]
        return chosen.reshape(KB).astype(jnp.int32)
    return jax.vmap(one_shard)(jax.random.split(jax.random.fold_in(key, 11), N_MP))


def draw_slots(key, part):

    def one_shard(shard_key):
        key_busy, key_rest, key_order = jax.random.split(shard_key, 3)
        busy = jax.random.randint(key_busy, (), 0, N_DP)
        rest = jax.random.permutation(key_rest, (N_DP - 1) * CAP)[:KB - CAP]
        owner = rest // CAP
        owner = owner + (owner >= busy).astype(jnp.int32)
        placed = owner * CAP + rest % CAP
        full = busy * CAP + jnp.arange(CAP, dtype=jnp.int32)
        every = jnp.concatenate([full.astype(jnp.int32), placed.astype(jnp.int32)])
        order = jax.random.permutation(key_order, KB)
        return every[order].astype(jnp.int32)
    return jax.vmap(one_shard)(jax.random.split(jax.random.fold_in(key, 23), N_MP))


def steps_of(rng, extent, shards, low, high):
    level, own = 1.0, jax.random.fold_in(rng, 6)
    for position, blocks in shards:
        draws = jnp.exp(jax.random.uniform(jax.random.fold_in(own, position), (blocks,), jnp.float32, low / len(shards), high / len(shards)))
        level = level * jnp.repeat(draws, extent[position] // blocks).reshape([-1 if axis == position else 1 for axis in range(len(extent))])
    return level


def noise(key, dims, deviation, reach, shards=(), kind=jnp.bfloat16):
    result = jax.random.normal(key, dims, jnp.float32) * deviation
    if len(shards) > 0:
        result = steps_of(key, dims, shards, -0.22, 0.18) * result
    return jnp.clip(result, min=-reach, max=reach).astype(kind)


def setup_inputs(seed: int = 0) -> dict:
    key_list = jax.random.split(jax.random.key(seed), 8)
    return {
        "x_in": draw_x_in(jax.random.fold_in(key_list[7], 71), 0),
        "gain": jnp.clip(1.0 + 0.15 * jax.random.normal(key_list[1], (D,), jnp.float32), 0.25, 1.75),
        "w_in": noise(key_list[2], (N_MP * KB, BLK * BLK), (D // DENS) ** -0.5, 0.5, ((0, 4),)),
        "w_out": noise(key_list[3], (N_MP * KB, BLK * BLK), (FF // N_MP // DENS) ** -0.5, 0.1875, ((0, 4),)),
        "grad_out": noise(key_list[4], (TOKENS, D), 1.0, 6.0, ((0, 128), (1, 4))),
        "block_cols": draw_block_cols(jax.random.fold_in(key_list[7], 71), 0),
        "slots": draw_slots(jax.random.fold_in(key_list[7], 71), 0),
    }


norm_eps = 1e-06
tanh_coef = 0.7978845608028654

def gelu_value(pre_act):
    cubic = pre_act * pre_act * pre_act
    slope_arg = jnp.tanh(tanh_coef * (pre_act + 0.044715 * cubic))
    return 0.5 * pre_act * (1.0 + slope_arg)

def gelu_slope(pre_act):
    cubic = pre_act * pre_act * pre_act
    slope_arg = jnp.tanh(tanh_coef * (pre_act + 0.044715 * cubic))
    inner = tanh_coef * (1.0 + 0.134145 * pre_act * pre_act)
    return 0.5 * (1.0 + slope_arg) + 0.5 * pre_act * (1.0 - slope_arg * slope_arg) * inner

def reference(x_in, gain, w_in, w_out, grad_out, block_cols, slots):
    in_all = w_in.astype(jnp.float32).reshape(N_MP, NRB, KR, BLK, BLK)
    out_all = w_out.astype(jnp.float32).reshape(N_MP, NRB, KR, BLK, BLK)
    weight_scale = 1.0 / math.sqrt(TOKENS)

    def step(totals, inputs):
        x_block, grad_block = inputs
        x_float = x_block.astype(jnp.float32)
        inv_rms = lax.rsqrt(lax.optimization_barrier(jnp.mean(x_float * x_float, axis=-1, keepdims=True)) + norm_eps)
        normed = (x_float * inv_rms * gain).astype(jnp.bfloat16)
        normed_rows = normed.astype(jnp.float32).reshape(TOK_DEV, NRB, BLK)
        grad_rows = grad_block.astype(jnp.float32).reshape(TOK_DEV, NRB, BLK)
        branch = jnp.zeros((TOK_DEV, NRB, BLK), jnp.float32)
        normed_grad = jnp.zeros((TOK_DEV, NRB, BLK), jnp.float32)
        pieces = []
        for shard in range(N_MP):
            col_ids = block_cols[shard].astype(jnp.int32)
            in_blocks = in_all[shard]
            out_blocks = out_all[shard]
            pre_parts = jnp.einsum('trb,rkbc->rktc', normed_rows, in_blocks)
            pre_act = jax.ops.segment_sum(pre_parts.reshape(KB, TOK_DEV, BLK), col_ids, num_segments=NCB)
            activation = gelu_value(pre_act).astype(jnp.bfloat16)
            act_blocks = jnp.take(activation, col_ids, axis=0).astype(jnp.float32).reshape(NRB, KR, TOK_DEV, BLK)
            branch = branch + jnp.einsum('rktc,rkcb->trb', act_blocks, out_blocks)
            act_parts = jnp.einsum('trb,rkcb->rktc', grad_rows, out_blocks)
            grad_act = jax.ops.segment_sum(act_parts.reshape(KB, TOK_DEV, BLK), col_ids, num_segments=NCB)
            grad_pre = (grad_act * gelu_slope(pre_act)).astype(jnp.bfloat16)
            pre_blocks = jnp.take(grad_pre, col_ids, axis=0).astype(jnp.float32).reshape(NRB, KR, TOK_DEV, BLK)
            normed_grad = normed_grad + jnp.einsum('rktc,rkbc->trb', pre_blocks, in_blocks)
            pieces.append(jnp.einsum('trb,rktc->rkcb', normed_rows, pre_blocks).reshape(KB, BLK * BLK))
        totals = totals + jnp.stack(pieces) * weight_scale
        return (totals, (branch.reshape(TOK_DEV, D).astype(jnp.bfloat16), normed_grad.reshape(TOK_DEV, D).astype(jnp.bfloat16)))
    start_totals = jnp.zeros((N_MP, KB, BLK * BLK), jnp.float32)
    inputs = (x_in.reshape(N_DP, TOK_DEV, D), grad_out.reshape(N_DP, TOK_DEV, D))
    totals, outputs = lax.scan(step, start_totals, inputs)
    branch, grad_normed = outputs
    shard_ids = jnp.arange(N_MP, dtype=jnp.int32)[:, None]
    owned_grad = jnp.zeros((N_MP, N_DP * CAP, BLK * BLK), jnp.float32).at[shard_ids, slots.astype(jnp.int32)].set(totals)
    return (branch.reshape(TOKENS, D), grad_normed.reshape(TOKENS, D), owned_grad)
```

```python
import functools
import math

import jax
import jax.numpy as jnp
from jax import lax
from jax.experimental import pallas as pl
from jax.experimental.pallas import tpu as pltpu
from jax.sharding import PartitionSpec as P

BLK = 64
NRB = 16
KR = 16
NCB = 128
TOK = 128
NX = 4
NZ = 16
NMP = 4
FWD = NZ // 2
BWD = NZ - 1 - FWD

norm_eps = 1e-06
tanh_coef = 0.7978845608028654
f32 = jnp.float32
bf16 = jnp.bfloat16
MESH = pl.DeviceIdType.MESH
NT = (((1,), (1,)), ((), ()))
TN = (((0,), (0,)), ((), ()))


def signal_all(peers):
    barrier = pltpu.get_barrier_semaphore()
    for peer in peers:
        pl.semaphore_signal(barrier, inc=1, device_id=peer, device_id_type=MESH)
    pl.semaphore_wait(barrier, len(peers))


def remote(src, dst, send, recv, peer):
    return pltpu.make_async_remote_copy(
        src_ref=src, dst_ref=dst, send_sem=send, recv_sem=recv,
        device_id=peer, device_id_type=MESH,
    )


def gather_kernel(x_ref, g_ref, xo_ref, go_ref, send, recv):
    me = lax.axis_index("mp")
    peers = [{"mp": lax.rem(me + i, NMP)} for i in range(1, NMP)]
    signal_all(peers)
    copies = []
    for i, peer in enumerate(peers):
        copies.append(remote(x_ref, xo_ref.at[me], send.at[0, i], recv.at[0, i], peer))
        copies.append(remote(g_ref, go_ref.at[me], send.at[1, i], recv.at[1, i], peer))
    for copy in copies:
        copy.start()
    xo_ref[me] = x_ref[...]
    go_ref[me] = g_ref[...]
    for copy in copies:
        copy.wait()


def gather_inputs(x_in, grad_out):
    whole = jax.ShapeDtypeStruct((NMP, TOK, x_in.shape[1]), bf16)
    vmem = pl.BlockSpec(memory_space=pltpu.VMEM)
    return pl.pallas_call(
        gather_kernel,
        out_shape=(whole, whole),
        in_specs=[vmem, vmem],
        out_specs=(vmem, vmem),
        scratch_shapes=[
            pltpu.SemaphoreType.DMA((2, NMP - 1)),
            pltpu.SemaphoreType.DMA((2, NMP - 1)),
        ],
        compiler_params=pltpu.CompilerParams(collective_id=0, has_side_effects=True),
        name="gather_inputs",
    )(x_in, grad_out)


def compute_kernel(scale, cols, slots, x_ref, g_ref, gain_ref, w_ref,
                   out_ref, branch_ref, gn_ref,
                   normed, pre, gact, act, gpre, parts, gath, halves, brt, gnt):
    squares = jnp.zeros((TOK, 1), f32)
    for p in range(NMP):
        xf = x_ref[p].astype(f32)
        squares += jnp.sum(xf * xf, axis=-1, keepdims=True)
    inv_rms = lax.rsqrt(squares / (NRB * BLK) + norm_eps)
    for p in range(NMP):
        normed[p] = (x_ref[p].astype(f32) * inv_rms * gain_ref[p]).astype(bf16)

    @pl.loop(0, NCB)
    def _(i):
        rows = pl.ds(pl.multiple_of(i * BLK, BLK), BLK)
        pre[rows, :] = jnp.zeros((BLK, TOK), f32)
        gact[rows, :] = jnp.zeros((BLK, TOK), f32)
        for j in range(4):
            out_ref[i * 4 + j] = jnp.zeros((BLK // 2, 2 * BLK), bf16)

    blank = jnp.zeros((TOK, BLK), bf16)

    def stacked(top, bottom):
        return jnp.concatenate([
            jnp.concatenate([top, blank], axis=1),
            jnp.concatenate([blank, bottom], axis=1),
        ], axis=0)

    @pl.loop(0, NMP)
    def _(p):
        for q in range(NRB // NMP):
            r = p * (NRB // NMP) + q
            lanes = slice(q * BLK, (q + 1) * BLK)
            both = stacked(normed[p, :, lanes], g_ref[p, :, lanes])
            rows = pl.ds(pl.multiple_of(r * KR * BLK, KR * BLK), KR * BLK)
            parts[...] = lax.dot_general(w_ref[rows, :], both, NT, preferred_element_type=f32)
            for k in range(KR):
                at = pl.ds(pl.multiple_of(cols[0, r * KR + k] * BLK, BLK), BLK)
                pre[at, :] += parts[k * BLK:(k + 1) * BLK, :TOK]
                gact[at, :] += parts[k * BLK:(k + 1) * BLK, TOK:]

    @pl.loop(0, NCB)
    def _(i):
        rows = pl.ds(pl.multiple_of(i * BLK, BLK), BLK)
        v = pre[rows, :]
        square = v * v
        th = jnp.tanh(tanh_coef * (v + 0.044715 * (square * v)))
        half = 0.5 * v
        act[rows, :] = (half * (1.0 + th)).astype(bf16)
        inner = tanh_coef * (1.0 + 0.134145 * square)
        slope = 0.5 * (1.0 + th) + half * (1.0 - th * th) * inner
        gpre[rows, :] = (gact[rows, :] * slope).astype(bf16)

    @pl.loop(0, NMP)
    def _(p):
        for q in range(NRB // NMP):
            r = p * (NRB // NMP) + q
            lanes = slice(q * BLK, (q + 1) * BLK)
            n_r = normed[p, :, lanes]
            for k in range(KR):
                at = pl.ds(pl.multiple_of(cols[0, r * KR + k] * BLK, BLK), BLK)
                block = gpre[at, :]
                gath[k * BLK:(k + 1) * BLK, :TOK] = block
                gath[k * BLK:(k + 1) * BLK, TOK:] = act[at, :]
                halves[k * 32:(k + 1) * 32, :TOK] = block[:32]
                halves[k * 32:(k + 1) * 32, TOK:] = block[32:]
            rows = pl.ds(pl.multiple_of(r * KR * BLK, KR * BLK), KR * BLK)
            sums = lax.dot_general(w_ref[rows, :], gath[...], TN, preferred_element_type=f32)
            at = pl.ds(pl.multiple_of(r * BLK, BLK), BLK)
            gnt[at, :] = sums[:BLK, :TOK]
            brt[at, :] = sums[BLK:, TOK:]
            grads = jnp.dot(halves[...], stacked(n_r, n_r), preferred_element_type=f32)
            grads = (grads * scale).astype(bf16)
            for k in range(KR):
                s = slots[0, r * KR + k]
                x, z, core, j = s // 128, (s // 8) % NZ, (s // 4) % 2, s % 4
                out_ref[((core * NZ + z) * NX + x) * 4 + j] = grads[k * 32:(k + 1) * 32]

    for p in range(NMP):
        rows = slice(p * 256, (p + 1) * 256)
        gn_ref[p] = gnt[rows, :].T.astype(bf16)
        branch_ref[p] = brt[rows, :].T.astype(bf16)


def compute(cols, slots, whole_x, whole_grad, gain, weights):
    vmem = pl.BlockSpec(memory_space=pltpu.VMEM)
    smem = pl.BlockSpec(memory_space=pltpu.SMEM)
    feats = jax.ShapeDtypeStruct((NMP, TOK, 256), bf16)
    scale = 1.0 / math.sqrt(TOK * 2 * NX * NZ)
    return pl.pallas_call(
        functools.partial(compute_kernel, scale),
        out_shape=(jax.ShapeDtypeStruct((512, BLK // 2, 2 * BLK), bf16), feats, feats),
        in_specs=[smem, smem, vmem, vmem, vmem, vmem],
        out_specs=(vmem, vmem, vmem),
        scratch_shapes=[
            pltpu.VMEM((NMP, TOK, 256), bf16),
            pltpu.VMEM((NCB * BLK, TOK), f32),
            pltpu.VMEM((NCB * BLK, TOK), f32),
            pltpu.VMEM((NCB * BLK, TOK), bf16),
            pltpu.VMEM((NCB * BLK, TOK), bf16),
            pltpu.VMEM((KR * BLK, 2 * TOK), f32),
            pltpu.VMEM((KR * BLK, 2 * TOK), bf16),
            pltpu.VMEM((KR * BLK // 2, 2 * TOK), bf16),
            pltpu.VMEM((NRB * BLK, TOK), f32),
            pltpu.VMEM((NRB * BLK, TOK), f32),
        ],
        compiler_params=pltpu.CompilerParams(vmem_limit_bytes=48 << 20),
        name="local_compute",
    )(cols, slots, whole_x, whole_grad, gain, weights)


def reduce_kernel(src, br_src, gn_src, owned, br_out, gn_out,
                  from_core, f_send, f_recv, b_send, b_recv, x_send, x_recv, m_recv,
                  core_ss, core_rs, f_ss, f_rs, b_ss, b_rs, x_ss, x_rs, m_ss, m_rs):
    dp, mp = lax.axis_index("dp"), lax.axis_index("mp")
    core = lax.rem(dp, 2)
    z = lax.rem(dp // 2, NZ)
    x = dp // (2 * NZ)

    def at(xx, zz, cc):
        return {"dp": (xx * NZ + zz) * 2 + cc}

    partner = at(x, z, 1 - core)
    ahead = at(x, lax.rem(z + 1, NZ), core)
    behind = at(x, lax.rem(z + NZ - 1, NZ), core)
    x_peers = [at(lax.rem(x + i, NX), z, core) for i in range(1, NX)]
    m_peers = [{"mp": lax.rem(mp + i, NMP)} for i in range(1, NMP)]
    signal_all([partner, ahead, behind] + x_peers + m_peers)

    def f_dest(s):
        return lax.rem(z + FWD - s, NZ)

    def b_dest(s):
        return lax.rem(z + NZ - BWD + s, NZ)

    core_copies = {}

    def core_copy(d):
        return remote(src.at[1 - core, d], from_core.at[d], core_ss.at[d], core_rs.at[d], partner)

    @pl.loop(0, FWD)
    def _(s):
        core_copy(f_dest(s)).start()

        @pl.when(s < BWD)
        def _():
            core_copy(b_dest(s)).start()

    core_copy(z).start()
    mp_copies = []
    for i, peer in enumerate(m_peers):
        to = lax.rem(mp + i + 1, NMP)
        mp_copies.append(remote(br_src.at[to], m_recv.at[0, i], m_ss.at[0, i], m_rs.at[0, i], peer))
        mp_copies.append(remote(gn_src.at[to], m_recv.at[1, i], m_ss.at[1, i], m_rs.at[1, i], peer))
    for copy in mp_copies:
        copy.start()

    def f_copy(s, q):
        return remote(f_send.at[s, q], f_recv.at[s, q], f_ss.at[s, q], f_rs.at[s, q], ahead)

    def b_copy(s, q):
        return remote(b_send.at[s, q], b_recv.at[s, q], b_ss.at[s, q], b_rs.at[s, q], behind)

    def pair(d, q):
        return src[core, d, q].astype(f32) + from_core[d, q].astype(f32)

    core_copy(f_dest(0)).wait_recv()
    for q in range(NX):
        f_send[0, q] = pair(f_dest(0), q).astype(bf16)
        f_copy(0, q).start()
    core_copy(b_dest(0)).wait_recv()
    for q in range(NX):
        b_send[0, q] = pair(b_dest(0), q).astype(bf16)
        b_copy(0, q).start()

    @pl.loop(1, FWD)
    def _(s):
        core_copy(f_dest(s)).wait_recv()

        @pl.when(s < BWD)
        def _():
            core_copy(b_dest(s)).wait_recv()

        for q in range(NX):
            f_copy(s - 1, q).wait_recv()
            f_send[s, q] = (pair(f_dest(s), q) + f_recv[s - 1, q].astype(f32)).astype(bf16)
            f_copy(s, q).start()

            @pl.when(s < BWD)
            def _():
                b_copy(s - 1, q).wait_recv()
                b_send[s, q] = (pair(b_dest(s), q) + b_recv[s - 1, q].astype(f32)).astype(bf16)
                b_copy(s, q).start()

    for o, (out, own_part) in enumerate(((br_out, br_src), (gn_out, gn_src))):
        total = own_part[mp].astype(f32)
        for i in range(NMP - 1):
            mp_copies[2 * i + o].wait_recv()
            total += m_recv[o, i].astype(f32)
        out[...] = total.astype(bf16)

    core_copy(z).wait_recv()
    for q in range(NX):
        b_copy(BWD - 1, q).wait_recv()
    for q in range(NX):
        f_copy(FWD - 1, q).wait_recv()

    def whole(q):
        return pair(z, q) + f_recv[FWD - 1, q].astype(f32) + b_recv[BWD - 1, q].astype(f32)

    x_copies = []
    for i, peer in enumerate(x_peers):
        x_send[i] = whole(lax.rem(x + i + 1, NX)).astype(bf16)
        copy = remote(x_send.at[i], x_recv.at[i], x_ss.at[i], x_rs.at[i], peer)
        copy.start()
        x_copies.append(copy)
    total = whole(x)
    for i in range(NX - 1):
        x_copies[i].wait_recv()
        total += x_recv[i].astype(f32)
    owned[...] = total

    for copy in x_copies + mp_copies:
        copy.wait_send()

    @pl.loop(0, NZ)
    def _(d):
        core_copy(d).wait_send()

    @pl.loop(0, FWD)
    def _(s):
        for q in range(NX):
            f_copy(s, q).wait_send()

            @pl.when(s < BWD)
            def _():
                b_copy(s, q).wait_send()


def reduce_all(outgoing, branch_parts, gn_parts):
    vmem = pl.BlockSpec(memory_space=pltpu.VMEM)
    dma = pltpu.SemaphoreType.DMA
    chunk = (NX, TOK, 128)
    feats = jax.ShapeDtypeStruct((TOK, 256), bf16)
    return pl.pallas_call(
        reduce_kernel,
        out_shape=(jax.ShapeDtypeStruct((TOK, 128), f32), feats, feats),
        in_specs=[vmem, vmem, vmem],
        out_specs=(vmem, vmem, vmem),
        scratch_shapes=[
            pltpu.VMEM((NZ,) + chunk, bf16),
            pltpu.VMEM((FWD,) + chunk, bf16),
            pltpu.VMEM((FWD,) + chunk, bf16),
            pltpu.VMEM((BWD,) + chunk, bf16),
            pltpu.VMEM((BWD,) + chunk, bf16),
            pltpu.VMEM((NX - 1, TOK, 128), bf16),
            pltpu.VMEM((NX - 1, TOK, 128), bf16),
            pltpu.VMEM((2, NMP - 1, TOK, 256), bf16),
            dma((NZ,)), dma((NZ,)),
            dma((FWD, NX)), dma((FWD, NX)),
            dma((BWD, NX)), dma((BWD, NX)),
            dma((NX - 1,)), dma((NX - 1,)),
            dma((2, NMP - 1)), dma((2, NMP - 1)),
        ],
        compiler_params=pltpu.CompilerParams(
            collective_id=1, has_side_effects=True, vmem_limit_bytes=40 << 20),
        name="reduce_all",
    )(outgoing.reshape(2, NZ, NX, TOK, 128), branch_parts, gn_parts)


def body(x_in, gain, w_in, w_out, grad_out, block_cols, slots):
    whole_x, whole_grad = gather_inputs(x_in, grad_out)
    weights = jnp.concatenate([
        w_in.reshape(-1, BLK, BLK).transpose(0, 2, 1),
        w_out.reshape(-1, BLK, BLK),
    ], axis=-1).reshape(-1, 2 * BLK)
    outgoing, branch_parts, gn_parts = compute(
        block_cols, slots, whole_x, whole_grad, gain.reshape(NMP, 1, 256), weights)
    owned, branch, grad_normed = reduce_all(outgoing, branch_parts, gn_parts)
    owned = owned.reshape(4, BLK // 2, 2, BLK).transpose(0, 2, 1, 3).reshape(1, 4, BLK * BLK)
    return (branch, grad_normed, owned)


def solution(mesh):
    placed = (
        P("dp", "mp"),
        P(),
        P("mp", None),
        P("mp", None),
        P("dp", "mp"),
        P("mp", None),
        P("mp", None),
    )
    return jax.shard_map(
        body,
        mesh=mesh,
        in_specs=placed,
        out_specs=(P("dp", "mp"), P("dp", "mp"), P("mp", "dp", None)),
        check_vma=False,
    )
```

```python
import functools
import math

import jax
import jax.numpy as jnp
from jax import lax
from jax.experimental import pallas as pl
from jax.experimental.pallas import tpu as pltpu
from jax.sharding import PartitionSpec as P

BLK = 64
NRB = 16
KR = 16
NCB = 128
TOK = 128
NX = 4
NZ = 16
NMP = 4
FWD = NZ // 2
BWD = NZ - 1 - FWD
RELAY_AT = 4

norm_eps = 1e-06
tanh_coef = 0.7978845608028654
f32 = jnp.float32
bf16 = jnp.bfloat16
MESH = pl.DeviceIdType.MESH
NT = (((1,), (1,)), ((), ()))
TN = (((0,), (0,)), ((), ()))


def signal_all(peers):
    barrier = pltpu.get_barrier_semaphore()
    for peer in peers:
        pl.semaphore_signal(barrier, inc=1, device_id=peer, device_id_type=MESH)
    pl.semaphore_wait(barrier, len(peers))


def remote(src, dst, send, recv, peer):
    return pltpu.make_async_remote_copy(
        src_ref=src, dst_ref=dst, send_sem=send, recv_sem=recv,
        device_id=peer, device_id_type=MESH,
    )


def gather_kernel(x_ref, g_ref, wi_hbm, wo_hbm, xo_ref, go_ref, w_ref,
                  wi, wo, s_in, s_out, send, recv, load):
    loads = [pltpu.make_async_copy(wi_hbm, wi, load.at[0]),
             pltpu.make_async_copy(wo_hbm, wo, load.at[1])]
    for copy in loads:
        copy.start()
    me = lax.axis_index("mp")
    nxt, prv = lax.rem(me + 1, NMP), lax.rem(me + NMP - 1, NMP)
    ahead, behind = {"mp": nxt}, {"mp": prv}
    signal_all([ahead, behind])
    x_ahead = remote(x_ref, xo_ref.at[me], send.at[0], recv.at[0], ahead)
    g_behind = remote(g_ref, go_ref.at[me], send.at[1], recv.at[1], behind)
    g_ahead = remote(g_ref, go_ref.at[me], send.at[2], recv.at[2], ahead)
    x_behind = remote(x_ref, xo_ref.at[me], send.at[3], recv.at[3], behind)
    x_relay = remote(xo_ref.at[prv], xo_ref.at[prv], send.at[4], recv.at[4], ahead)
    g_relay = remote(go_ref.at[nxt], go_ref.at[nxt], send.at[5], recv.at[5], behind)
    for copy in (x_ahead, g_behind, g_ahead, x_behind):
        copy.start()
    xo_ref[me] = x_ref[...]
    go_ref[me] = g_ref[...]
    for copy in loads:
        copy.wait()
    low = lax.broadcasted_iota(jnp.int32, (8, 2 * BLK), 1) < BLK

    def relayout(r):
        top = pl.ds(pl.multiple_of(r * KR, KR), KR)
        for j in range(BLK // 2):
            lanes = slice(j * 2 * BLK, (j + 1) * 2 * BLK)
            v = wi[top, lanes].astype(f32)
            a, b = v[:8], v[8:]
            s_in[pl.ds(2 * j, 8, stride=BLK), :] = jnp.where(low, a, pltpu.roll(b, BLK, 1))
            s_in[pl.ds(2 * j + 1, 8, stride=BLK), :] = jnp.where(low, pltpu.roll(a, BLK, 1), b)
            v = wo[top, lanes].astype(f32)
            for h in range(2):
                u = v[h * 8:h * 8 + 8]
                s_out[pl.ds(h * 8 * BLK + 2 * j, 8, stride=BLK), :] = pltpu.roll(u, BLK, 1)
                s_out[pl.ds(h * 8 * BLK + 2 * j + 1, 8, stride=BLK), :] = u
        for k in range(8):
            turned = s_in[k * BLK:(k + 1) * BLK, :].T
            for h in range(2):
                kk = h * 8 + k
                both = jnp.concatenate([
                    turned[h * BLK:(h + 1) * BLK],
                    s_out[kk * BLK:(kk + 1) * BLK, BLK:],
                ], axis=1)
                w_ref[pl.ds(pl.multiple_of((r * KR + kk) * BLK, BLK), BLK), :] = both.astype(bf16)

    pl.loop(0, RELAY_AT)(relayout)
    x_ahead.wait_recv()
    x_relay.start()
    g_behind.wait_recv()
    g_relay.start()
    pl.loop(RELAY_AT, NRB)(relayout)
    for copy in (g_ahead, x_behind, x_relay, g_relay):
        copy.wait_recv()
    for copy in (x_ahead, g_behind, g_ahead, x_behind, x_relay, g_relay):
        copy.wait_send()


def gather_inputs(x_in, grad_out, w_in, w_out):
    whole = jax.ShapeDtypeStruct((NMP, TOK, x_in.shape[1]), bf16)
    vmem = pl.BlockSpec(memory_space=pltpu.VMEM)
    hbm = pl.BlockSpec(memory_space=pl.ANY)
    return pl.pallas_call(
        gather_kernel,
        out_shape=(whole, whole, jax.ShapeDtypeStruct((NRB * KR * BLK, 2 * BLK), bf16)),
        in_specs=[vmem, vmem, hbm, hbm],
        out_specs=(vmem, vmem, vmem),
        scratch_shapes=[
            pltpu.VMEM(w_in.shape, bf16),
            pltpu.VMEM(w_out.shape, bf16),
            pltpu.VMEM((KR * BLK // 2, 2 * BLK), f32),
            pltpu.VMEM((KR * BLK, 2 * BLK), f32),
            pltpu.SemaphoreType.DMA((6,)),
            pltpu.SemaphoreType.DMA((6,)),
            pltpu.SemaphoreType.DMA((2,)),
        ],
        compiler_params=pltpu.CompilerParams(
            collective_id=0, has_side_effects=True, vmem_limit_bytes=40 << 20),
        name="gather_inputs",
    )(x_in, grad_out, w_in, w_out)


def compute_kernel(scale, cols, slots, x_ref, g_ref, gain_ref, w_ref,
                   out_ref, branch_ref, gn_ref,
                   normed, pre, gact, act, gpre, parts, gath, halves, brt, gnt):
    squares = jnp.zeros((TOK, 1), f32)
    for p in range(NMP):
        xf = x_ref[p].astype(f32)
        squares += jnp.sum(xf * xf, axis=-1, keepdims=True)
    inv_rms = lax.rsqrt(squares / (NRB * BLK) + norm_eps)
    for p in range(NMP):
        normed[p] = (x_ref[p].astype(f32) * inv_rms * gain_ref[p]).astype(bf16)

    @pl.loop(0, NCB)
    def _(i):
        rows = pl.ds(pl.multiple_of(i * BLK, BLK), BLK)
        pre[rows, :] = jnp.zeros((BLK, TOK), f32)
        gact[rows, :] = jnp.zeros((BLK, TOK), f32)
        for j in range(4):
            out_ref[i * 4 + j] = jnp.zeros((BLK // 2, 2 * BLK), bf16)

    blank = jnp.zeros((TOK, BLK), bf16)

    def stacked(top, bottom):
        return jnp.concatenate([
            jnp.concatenate([top, blank], axis=1),
            jnp.concatenate([blank, bottom], axis=1),
        ], axis=0)

    @pl.loop(0, NMP)
    def _(p):
        for q in range(NRB // NMP):
            r = p * (NRB // NMP) + q
            lanes = slice(q * BLK, (q + 1) * BLK)
            both = stacked(normed[p, :, lanes], g_ref[p, :, lanes])
            rows = pl.ds(pl.multiple_of(r * KR * BLK, KR * BLK), KR * BLK)
            parts[...] = lax.dot_general(w_ref[rows, :], both, NT, preferred_element_type=f32)
            for k in range(KR):
                at = pl.ds(pl.multiple_of(cols[0, r * KR + k] * BLK, BLK), BLK)
                pre[at, :] += parts[k * BLK:(k + 1) * BLK, :TOK]
                gact[at, :] += parts[k * BLK:(k + 1) * BLK, TOK:]

    @pl.loop(0, NCB)
    def _(i):
        rows = pl.ds(pl.multiple_of(i * BLK, BLK), BLK)
        v = pre[rows, :]
        square = v * v
        th = jnp.tanh(tanh_coef * (v + 0.044715 * (square * v)))
        half = 0.5 * v
        act[rows, :] = (half * (1.0 + th)).astype(bf16)
        inner = tanh_coef * (1.0 + 0.134145 * square)
        slope = 0.5 * (1.0 + th) + half * (1.0 - th * th) * inner
        gpre[rows, :] = (gact[rows, :] * slope).astype(bf16)

    @pl.loop(0, NMP)
    def _(p):
        for q in range(NRB // NMP):
            r = p * (NRB // NMP) + q
            lanes = slice(q * BLK, (q + 1) * BLK)
            n_r = normed[p, :, lanes]
            for k in range(KR):
                at = pl.ds(pl.multiple_of(cols[0, r * KR + k] * BLK, BLK), BLK)
                block = gpre[at, :]
                gath[k * BLK:(k + 1) * BLK, :TOK] = block
                gath[k * BLK:(k + 1) * BLK, TOK:] = act[at, :]
                halves[k * 32:(k + 1) * 32, :TOK] = block[:32]
                halves[k * 32:(k + 1) * 32, TOK:] = block[32:]
            rows = pl.ds(pl.multiple_of(r * KR * BLK, KR * BLK), KR * BLK)
            sums = lax.dot_general(w_ref[rows, :], gath[...], TN, preferred_element_type=f32)
            at = pl.ds(pl.multiple_of(r * BLK, BLK), BLK)
            gnt[at, :] = sums[:BLK, :TOK]
            brt[at, :] = sums[BLK:, TOK:]
            grads = jnp.dot(halves[...], stacked(n_r, n_r), preferred_element_type=f32)
            grads = (grads * scale).astype(bf16)
            for k in range(KR):
                s = slots[0, r * KR + k]
                x, z, core, j = s // 128, (s // 8) % NZ, (s // 4) % 2, s % 4
                out_ref[((core * NZ + z) * NX + x) * 4 + j] = grads[k * 32:(k + 1) * 32]

    for p in range(NMP):
        rows = slice(p * 256, (p + 1) * 256)
        gn_ref[p] = gnt[rows, :].T.astype(bf16)
        branch_ref[p] = brt[rows, :].T.astype(bf16)


def compute(cols, slots, whole_x, whole_grad, gain, weights):
    vmem = pl.BlockSpec(memory_space=pltpu.VMEM)
    smem = pl.BlockSpec(memory_space=pltpu.SMEM)
    feats = jax.ShapeDtypeStruct((NMP, TOK, 256), bf16)
    scale = 1.0 / math.sqrt(TOK * 2 * NX * NZ)
    return pl.pallas_call(
        functools.partial(compute_kernel, scale),
        out_shape=(jax.ShapeDtypeStruct((512, BLK // 2, 2 * BLK), bf16), feats, feats),
        in_specs=[smem, smem, vmem, vmem, vmem, vmem],
        out_specs=(vmem, vmem, vmem),
        scratch_shapes=[
            pltpu.VMEM((NMP, TOK, 256), bf16),
            pltpu.VMEM((NCB * BLK, TOK), f32),
            pltpu.VMEM((NCB * BLK, TOK), f32),
            pltpu.VMEM((NCB * BLK, TOK), bf16),
            pltpu.VMEM((NCB * BLK, TOK), bf16),
            pltpu.VMEM((KR * BLK, 2 * TOK), f32),
            pltpu.VMEM((KR * BLK, 2 * TOK), bf16),
            pltpu.VMEM((KR * BLK // 2, 2 * TOK), bf16),
            pltpu.VMEM((NRB * BLK, TOK), f32),
            pltpu.VMEM((NRB * BLK, TOK), f32),
        ],
        compiler_params=pltpu.CompilerParams(vmem_limit_bytes=48 << 20),
        name="local_compute",
    )(cols, slots, whole_x, whole_grad, gain, weights)


def reduce_kernel(src, br_src, gn_src, owned, br_out, gn_out,
                  from_core, f_send, f_recv, b_send, b_recv, x_send, x_recv, m_recv,
                  core_ss, core_rs, f_ss, f_rs, b_ss, b_rs, x_ss, x_rs, m_ss, m_rs):
    dp, mp = lax.axis_index("dp"), lax.axis_index("mp")
    core = lax.rem(dp, 2)
    z = lax.rem(dp // 2, NZ)
    x = dp // (2 * NZ)

    def at(xx, zz, cc):
        return {"dp": (xx * NZ + zz) * 2 + cc}

    partner = at(x, z, 1 - core)
    ahead = at(x, lax.rem(z + 1, NZ), core)
    behind = at(x, lax.rem(z + NZ - 1, NZ), core)
    x_peers = [at(lax.rem(x + i, NX), z, core) for i in range(1, NX)]
    m_peers = [{"mp": lax.rem(mp + i, NMP)} for i in range(1, NMP)]
    signal_all([partner, ahead, behind] + x_peers + m_peers)

    def f_dest(s):
        return lax.rem(z + FWD - s, NZ)

    def b_dest(s):
        return lax.rem(z + NZ - BWD + s, NZ)

    core_copies = {}

    def core_copy(d):
        return remote(src.at[1 - core, d], from_core.at[d], core_ss.at[d], core_rs.at[d], partner)

    @pl.loop(0, FWD)
    def _(s):
        core_copy(f_dest(s)).start()

        @pl.when(s < BWD)
        def _():
            core_copy(b_dest(s)).start()

    core_copy(z).start()
    mp_copies = []
    for i, peer in enumerate(m_peers):
        to = lax.rem(mp + i + 1, NMP)
        mp_copies.append(remote(br_src.at[to], m_recv.at[0, i], m_ss.at[0, i], m_rs.at[0, i], peer))
        mp_copies.append(remote(gn_src.at[to], m_recv.at[1, i], m_ss.at[1, i], m_rs.at[1, i], peer))
    for copy in mp_copies:
        copy.start()

    def f_copy(s, q):
        return remote(f_send.at[s, q], f_recv.at[s, q], f_ss.at[s, q], f_rs.at[s, q], ahead)

    def b_copy(s, q):
        return remote(b_send.at[s, q], b_recv.at[s, q], b_ss.at[s, q], b_rs.at[s, q], behind)

    def pair(d, q):
        return src[core, d, q].astype(f32) + from_core[d, q].astype(f32)

    core_copy(f_dest(0)).wait_recv()
    for q in range(NX):
        f_send[0, q] = pair(f_dest(0), q).astype(bf16)
        f_copy(0, q).start()
    core_copy(b_dest(0)).wait_recv()
    for q in range(NX):
        b_send[0, q] = pair(b_dest(0), q).astype(bf16)
        b_copy(0, q).start()

    @pl.loop(1, FWD)
    def _(s):
        core_copy(f_dest(s)).wait_recv()

        @pl.when(s < BWD)
        def _():
            core_copy(b_dest(s)).wait_recv()

        for q in range(NX):
            f_copy(s - 1, q).wait_recv()
            f_send[s, q] = (pair(f_dest(s), q) + f_recv[s - 1, q].astype(f32)).astype(bf16)
            f_copy(s, q).start()

            @pl.when(s < BWD)
            def _():
                b_copy(s - 1, q).wait_recv()
                b_send[s, q] = (pair(b_dest(s), q) + b_recv[s - 1, q].astype(f32)).astype(bf16)
                b_copy(s, q).start()

    for o, (out, own_part) in enumerate(((br_out, br_src), (gn_out, gn_src))):
        total = own_part[mp].astype(f32)
        for i in range(NMP - 1):
            mp_copies[2 * i + o].wait_recv()
            total += m_recv[o, i].astype(f32)
        out[...] = total.astype(bf16)

    core_copy(z).wait_recv()
    for q in range(NX):
        b_copy(BWD - 1, q).wait_recv()
    for q in range(NX):
        f_copy(FWD - 1, q).wait_recv()

    def whole(q):
        return pair(z, q) + f_recv[FWD - 1, q].astype(f32) + b_recv[BWD - 1, q].astype(f32)

    x_copies = []
    for i, peer in enumerate(x_peers):
        x_send[i] = whole(lax.rem(x + i + 1, NX)).astype(bf16)
        copy = remote(x_send.at[i], x_recv.at[i], x_ss.at[i], x_rs.at[i], peer)
        copy.start()
        x_copies.append(copy)
    total = whole(x)
    for i in range(NX - 1):
        x_copies[i].wait_recv()
        total += x_recv[i].astype(f32)
    owned[...] = total

    for copy in x_copies + mp_copies:
        copy.wait_send()

    @pl.loop(0, NZ)
    def _(d):
        core_copy(d).wait_send()

    @pl.loop(0, FWD)
    def _(s):
        for q in range(NX):
            f_copy(s, q).wait_send()

            @pl.when(s < BWD)
            def _():
                b_copy(s, q).wait_send()


def reduce_all(outgoing, branch_parts, gn_parts):
    vmem = pl.BlockSpec(memory_space=pltpu.VMEM)
    dma = pltpu.SemaphoreType.DMA
    chunk = (NX, TOK, 128)
    feats = jax.ShapeDtypeStruct((TOK, 256), bf16)
    return pl.pallas_call(
        reduce_kernel,
        out_shape=(jax.ShapeDtypeStruct((TOK, 128), f32), feats, feats),
        in_specs=[vmem, vmem, vmem],
        out_specs=(vmem, vmem, vmem),
        scratch_shapes=[
            pltpu.VMEM((NZ,) + chunk, bf16),
            pltpu.VMEM((FWD,) + chunk, bf16),
            pltpu.VMEM((FWD,) + chunk, bf16),
            pltpu.VMEM((BWD,) + chunk, bf16),
            pltpu.VMEM((BWD,) + chunk, bf16),
            pltpu.VMEM((NX - 1, TOK, 128), bf16),
            pltpu.VMEM((NX - 1, TOK, 128), bf16),
            pltpu.VMEM((2, NMP - 1, TOK, 256), bf16),
            dma((NZ,)), dma((NZ,)),
            dma((FWD, NX)), dma((FWD, NX)),
            dma((BWD, NX)), dma((BWD, NX)),
            dma((NX - 1,)), dma((NX - 1,)),
            dma((2, NMP - 1)), dma((2, NMP - 1)),
        ],
        compiler_params=pltpu.CompilerParams(
            collective_id=1, has_side_effects=True, vmem_limit_bytes=40 << 20),
        name="reduce_all",
    )(outgoing.reshape(2, NZ, NX, TOK, 128), branch_parts, gn_parts)


def body(x_in, gain, w_in, w_out, grad_out, block_cols, slots):
    whole_x, whole_grad, weights = gather_inputs(x_in, grad_out, w_in, w_out)
    outgoing, branch_parts, gn_parts = compute(
        block_cols, slots, whole_x, whole_grad, gain.reshape(NMP, 1, 256), weights)
    owned, branch, grad_normed = reduce_all(outgoing, branch_parts, gn_parts)
    owned = owned.reshape(4, BLK // 2, 2, BLK).transpose(0, 2, 1, 3).reshape(1, 4, BLK * BLK)
    return (branch, grad_normed, owned)


def solution(mesh):
    placed = (
        P("dp", "mp"),
        P(),
        P("mp", None),
        P("mp", None),
        P("dp", "mp"),
        P("mp", None),
        P("mp", None),
    )
    return jax.shard_map(
        body,
        mesh=mesh,
        in_specs=placed,
        out_specs=(P("dp", "mp"), P("dp", "mp"), P("mp", "dp", None)),
        check_vma=False,
    )
```

```python
import functools
import math

import jax
import jax.numpy as jnp
from jax import lax
from jax.experimental import pallas as pl
from jax.experimental.pallas import tpu as pltpu
from jax.sharding import PartitionSpec as P

BLK = 64
NRB = 16
KR = 16
NCB = 128
TOK = 128
NX = 4
NZ = 16
NMP = 4
FWD = NZ // 2
BWD = NZ - 1 - FWD
RELAY_AT = 4

norm_eps = 1e-06
tanh_coef = 0.7978845608028654
f32 = jnp.float32
bf16 = jnp.bfloat16
MESH = pl.DeviceIdType.MESH
NT = (((1,), (1,)), ((), ()))
TN = (((0,), (0,)), ((), ()))


def signal_all(peers):
    barrier = pltpu.get_barrier_semaphore()
    for peer in peers:
        pl.semaphore_signal(barrier, inc=1, device_id=peer, device_id_type=MESH)
    pl.semaphore_wait(barrier, len(peers))


def remote(src, dst, send, recv, peer):
    return pltpu.make_async_remote_copy(
        src_ref=src, dst_ref=dst, send_sem=send, recv_sem=recv,
        device_id=peer, device_id_type=MESH,
    )


def gather_kernel(x_ref, g_ref, wi_hbm, wo_hbm, xo_ref, go_ref, w_ref,
                  wi, wo, s_in, s_out, send, recv, load):
    me = lax.axis_index("mp")
    loads = [pltpu.make_async_copy(wi_hbm, wi, load.at[0]),
             pltpu.make_async_copy(wo_hbm, wo, load.at[1]),
             pltpu.make_async_copy(x_ref, xo_ref.at[me], load.at[2]),
             pltpu.make_async_copy(g_ref, go_ref.at[me], load.at[3])]
    for copy in loads:
        copy.start()
    nxt, prv = lax.rem(me + 1, NMP), lax.rem(me + NMP - 1, NMP)
    ahead, behind = {"mp": nxt}, {"mp": prv}
    signal_all([ahead, behind])
    x_ahead = remote(x_ref, xo_ref.at[me], send.at[0], recv.at[0], ahead)
    g_behind = remote(g_ref, go_ref.at[me], send.at[1], recv.at[1], behind)
    g_ahead = remote(g_ref, go_ref.at[me], send.at[2], recv.at[2], ahead)
    x_behind = remote(x_ref, xo_ref.at[me], send.at[3], recv.at[3], behind)
    x_relay = remote(xo_ref.at[prv], xo_ref.at[prv], send.at[4], recv.at[4], ahead)
    g_relay = remote(go_ref.at[nxt], go_ref.at[nxt], send.at[5], recv.at[5], behind)
    for copy in (x_ahead, g_behind, g_ahead, x_behind):
        copy.start()
    for copy in loads:
        copy.wait()
    low = lax.broadcasted_iota(jnp.int32, (8, 2 * BLK), 1) < BLK
    square = (2 * BLK, 2 * BLK)
    eye = (lax.broadcasted_iota(jnp.int32, square, 0)
           == lax.broadcasted_iota(jnp.int32, square, 1)).astype(f32).astype(bf16)

    def relayout(r):
        top = pl.ds(pl.multiple_of(r * KR, KR), KR)
        for j in range(BLK // 2):
            lanes = slice(j * 2 * BLK, (j + 1) * 2 * BLK)
            v = wi[top, lanes].astype(f32)
            a, b = v[:8], v[8:]
            s_in[pl.ds(2 * j, 8, stride=BLK), :] = jnp.where(low, a, pltpu.roll(b, BLK, 1))
            s_in[pl.ds(2 * j + 1, 8, stride=BLK), :] = jnp.where(low, pltpu.roll(a, BLK, 1), b)
            v = wo[top, lanes].astype(f32)
            for h in range(2):
                u = v[h * 8:h * 8 + 8]
                s_out[pl.ds(h * 8 * BLK + 2 * j, 8, stride=BLK), :] = pltpu.roll(u, BLK, 1)
                s_out[pl.ds(h * 8 * BLK + 2 * j + 1, 8, stride=BLK), :] = u
        for k in range(8):
            turned = lax.dot_general(
                eye, s_in[k * BLK:(k + 1) * BLK, :].astype(bf16), NT, preferred_element_type=f32)
            for h in range(2):
                kk = h * 8 + k
                both = jnp.concatenate([
                    turned[h * BLK:(h + 1) * BLK],
                    s_out[kk * BLK:(kk + 1) * BLK, BLK:],
                ], axis=1)
                w_ref[pl.ds(pl.multiple_of((r * KR + kk) * BLK, BLK), BLK), :] = both.astype(bf16)

    pl.loop(0, RELAY_AT)(relayout)
    x_ahead.wait_recv()
    x_relay.start()
    g_behind.wait_recv()
    g_relay.start()
    pl.loop(RELAY_AT, NRB)(relayout)
    for copy in (g_ahead, x_behind, x_relay, g_relay):
        copy.wait_recv()
    for copy in (x_ahead, g_behind, g_ahead, x_behind, x_relay, g_relay):
        copy.wait_send()


def gather_inputs(x_in, grad_out, w_in, w_out):
    whole = jax.ShapeDtypeStruct((NMP, TOK, x_in.shape[1]), bf16)
    vmem = pl.BlockSpec(memory_space=pltpu.VMEM)
    hbm = pl.BlockSpec(memory_space=pltpu.HBM)
    return pl.pallas_call(
        gather_kernel,
        out_shape=(whole, whole, jax.ShapeDtypeStruct((NRB * KR * BLK, 2 * BLK), bf16)),
        in_specs=[hbm, hbm, hbm, hbm],
        out_specs=(vmem, vmem, vmem),
        scratch_shapes=[
            pltpu.VMEM(w_in.shape, bf16),
            pltpu.VMEM(w_out.shape, bf16),
            pltpu.VMEM((KR * BLK // 2, 2 * BLK), f32),
            pltpu.VMEM((KR * BLK, 2 * BLK), f32),
            pltpu.SemaphoreType.DMA((6,)),
            pltpu.SemaphoreType.DMA((6,)),
            pltpu.SemaphoreType.DMA((4,)),
        ],
        compiler_params=pltpu.CompilerParams(
            collective_id=0, has_side_effects=True, vmem_limit_bytes=16 << 20),
        name="gather_inputs",
    )(*(pltpu.with_memory_space_constraint(a, pltpu.HBM) for a in (x_in, grad_out, w_in, w_out)))


def compute_kernel(scale, cols, slots, x_ref, g_ref, gain_ref, w_ref,
                   out_ref, branch_ref, gn_ref,
                   normed, pre, gact, act, gpre, parts, gath, halves, brt, gnt):
    squares = jnp.zeros((TOK, 1), f32)
    for p in range(NMP):
        xf = x_ref[p].astype(f32)
        squares += jnp.sum(xf * xf, axis=-1, keepdims=True)
    inv_rms = lax.rsqrt(squares / (NRB * BLK) + norm_eps)
    for p in range(NMP):
        normed[p] = (x_ref[p].astype(f32) * inv_rms * gain_ref[p]).astype(bf16)

    @pl.loop(0, NCB)
    def _(i):
        rows = pl.ds(pl.multiple_of(i * BLK, BLK), BLK)
        pre[rows, :] = jnp.zeros((BLK, TOK), f32)
        gact[rows, :] = jnp.zeros((BLK, TOK), f32)
        for j in range(4):
            out_ref[i * 4 + j] = jnp.zeros((BLK // 2, 2 * BLK), bf16)

    blank = jnp.zeros((TOK, BLK), bf16)

    def stacked(top, bottom):
        return jnp.concatenate([
            jnp.concatenate([top, blank], axis=1),
            jnp.concatenate([blank, bottom], axis=1),
        ], axis=0)

    @pl.loop(0, NMP)
    def _(p):
        for q in range(NRB // NMP):
            r = p * (NRB // NMP) + q
            lanes = slice(q * BLK, (q + 1) * BLK)
            both = stacked(normed[p, :, lanes], g_ref[p, :, lanes])
            rows = pl.ds(pl.multiple_of(r * KR * BLK, KR * BLK), KR * BLK)
            parts[...] = lax.dot_general(w_ref[rows, :], both, NT, preferred_element_type=f32)
            for k in range(KR):
                at = pl.ds(pl.multiple_of(cols[0, r * KR + k] * BLK, BLK), BLK)
                pre[at, :] += parts[k * BLK:(k + 1) * BLK, :TOK]
                gact[at, :] += parts[k * BLK:(k + 1) * BLK, TOK:]

    @pl.loop(0, NCB)
    def _(i):
        rows = pl.ds(pl.multiple_of(i * BLK, BLK), BLK)
        v = pre[rows, :]
        square = v * v
        th = jnp.tanh(tanh_coef * (v + 0.044715 * (square * v)))
        half = 0.5 * v
        act[rows, :] = (half * (1.0 + th)).astype(bf16)
        inner = tanh_coef * (1.0 + 0.134145 * square)
        slope = 0.5 * (1.0 + th) + half * (1.0 - th * th) * inner
        gpre[rows, :] = (gact[rows, :] * slope).astype(bf16)

    @pl.loop(0, NMP)
    def _(p):
        for q in range(NRB // NMP):
            r = p * (NRB // NMP) + q
            lanes = slice(q * BLK, (q + 1) * BLK)
            n_r = normed[p, :, lanes]
            for k in range(KR):
                at = pl.ds(pl.multiple_of(cols[0, r * KR + k] * BLK, BLK), BLK)
                block = gpre[at, :]
                gath[k * BLK:(k + 1) * BLK, :TOK] = block
                gath[k * BLK:(k + 1) * BLK, TOK:] = act[at, :]
                halves[k * 32:(k + 1) * 32, :TOK] = block[:32]
                halves[k * 32:(k + 1) * 32, TOK:] = block[32:]
            rows = pl.ds(pl.multiple_of(r * KR * BLK, KR * BLK), KR * BLK)
            sums = lax.dot_general(w_ref[rows, :], gath[...], TN, preferred_element_type=f32)
            at = pl.ds(pl.multiple_of(r * BLK, BLK), BLK)
            gnt[at, :] = sums[:BLK, :TOK]
            brt[at, :] = sums[BLK:, TOK:]
            grads = jnp.dot(halves[...], stacked(n_r, n_r), preferred_element_type=f32)
            grads = (grads * scale).astype(bf16)
            for k in range(KR):
                s = slots[0, r * KR + k]
                x, z, core, j = s // 128, (s // 8) % NZ, (s // 4) % 2, s % 4
                out_ref[((core * NZ + z) * NX + x) * 4 + j] = grads[k * 32:(k + 1) * 32]

    for p in range(NMP):
        rows = slice(p * 256, (p + 1) * 256)
        gn_ref[p] = gnt[rows, :].T.astype(bf16)
        branch_ref[p] = brt[rows, :].T.astype(bf16)


def compute(cols, slots, whole_x, whole_grad, gain, weights):
    vmem = pl.BlockSpec(memory_space=pltpu.VMEM)
    smem = pl.BlockSpec(memory_space=pltpu.SMEM)
    feats = jax.ShapeDtypeStruct((NMP, TOK, 256), bf16)
    scale = 1.0 / math.sqrt(TOK * 2 * NX * NZ)
    return pl.pallas_call(
        functools.partial(compute_kernel, scale),
        out_shape=(jax.ShapeDtypeStruct((512, BLK // 2, 2 * BLK), bf16), feats, feats),
        in_specs=[smem, smem, vmem, vmem, vmem, vmem],
        out_specs=(vmem, vmem, vmem),
        scratch_shapes=[
            pltpu.VMEM((NMP, TOK, 256), bf16),
            pltpu.VMEM((NCB * BLK, TOK), f32),
            pltpu.VMEM((NCB * BLK, TOK), f32),
            pltpu.VMEM((NCB * BLK, TOK), bf16),
            pltpu.VMEM((NCB * BLK, TOK), bf16),
            pltpu.VMEM((KR * BLK, 2 * TOK), f32),
            pltpu.VMEM((KR * BLK, 2 * TOK), bf16),
            pltpu.VMEM((KR * BLK // 2, 2 * TOK), bf16),
            pltpu.VMEM((NRB * BLK, TOK), f32),
            pltpu.VMEM((NRB * BLK, TOK), f32),
        ],
        compiler_params=pltpu.CompilerParams(vmem_limit_bytes=24 << 20),
        name="local_compute",
    )(cols, slots, whole_x, whole_grad, gain, weights)


def reduce_kernel(src, br_src, gn_src, owned, br_out, gn_out,
                  from_core, f_send, f_recv, b_send, b_recv, x_send, x_recv, m_recv,
                  core_ss, core_rs, f_ss, f_rs, b_ss, b_rs, x_ss, x_rs, m_ss, m_rs):
    dp, mp = lax.axis_index("dp"), lax.axis_index("mp")
    core = lax.rem(dp, 2)
    z = lax.rem(dp // 2, NZ)
    x = dp // (2 * NZ)

    def at(xx, zz, cc):
        return {"dp": (xx * NZ + zz) * 2 + cc}

    partner = at(x, z, 1 - core)
    ahead = at(x, lax.rem(z + 1, NZ), core)
    behind = at(x, lax.rem(z + NZ - 1, NZ), core)
    x_peers = [at(lax.rem(x + i, NX), z, core) for i in range(1, NX)]
    m_peers = [{"mp": lax.rem(mp + i, NMP)} for i in range(1, NMP)]
    signal_all([partner, ahead, behind] + x_peers + m_peers)

    def f_dest(s):
        return lax.rem(z + FWD - s, NZ)

    def b_dest(s):
        return lax.rem(z + NZ - BWD + s, NZ)

    core_copies = {}

    def core_copy(d):
        return remote(src.at[1 - core, d], from_core.at[d], core_ss.at[d], core_rs.at[d], partner)

    @pl.loop(0, FWD)
    def _(s):
        core_copy(f_dest(s)).start()

        @pl.when(s < BWD)
        def _():
            core_copy(b_dest(s)).start()

    core_copy(z).start()
    mp_copies = []
    for i, peer in enumerate(m_peers):
        to = lax.rem(mp + i + 1, NMP)
        mp_copies.append(remote(br_src.at[to], m_recv.at[0, i], m_ss.at[0, i], m_rs.at[0, i], peer))
        mp_copies.append(remote(gn_src.at[to], m_recv.at[1, i], m_ss.at[1, i], m_rs.at[1, i], peer))
    for copy in mp_copies:
        copy.start()

    def f_copy(s, q):
        return remote(f_send.at[s, q], f_recv.at[s, q], f_ss.at[s, q], f_rs.at[s, q], ahead)

    def b_copy(s, q):
        return remote(b_send.at[s, q], b_recv.at[s, q], b_ss.at[s, q], b_rs.at[s, q], behind)

    def pair(d, q):
        return src[core, d, q].astype(f32) + from_core[d, q].astype(f32)

    core_copy(f_dest(0)).wait_recv()
    for q in range(NX):
        f_send[0, q] = pair(f_dest(0), q).astype(bf16)
        f_copy(0, q).start()
    core_copy(b_dest(0)).wait_recv()
    for q in range(NX):
        b_send[0, q] = pair(b_dest(0), q).astype(bf16)
        b_copy(0, q).start()

    @pl.loop(1, FWD)
    def _(s):
        core_copy(f_dest(s)).wait_recv()

        @pl.when(s < BWD)
        def _():
            core_copy(b_dest(s)).wait_recv()

        for q in range(NX):
            f_copy(s - 1, q).wait_recv()
            f_send[s, q] = (pair(f_dest(s), q) + f_recv[s - 1, q].astype(f32)).astype(bf16)
            f_copy(s, q).start()

            @pl.when(s < BWD)
            def _():
                b_copy(s - 1, q).wait_recv()
                b_send[s, q] = (pair(b_dest(s), q) + b_recv[s - 1, q].astype(f32)).astype(bf16)
                b_copy(s, q).start()

    for o, (out, own_part) in enumerate(((br_out, br_src), (gn_out, gn_src))):
        total = own_part[mp].astype(f32)
        for i in range(NMP - 1):
            mp_copies[2 * i + o].wait_recv()
            total += m_recv[o, i].astype(f32)
        out[...] = total.astype(bf16)

    core_copy(z).wait_recv()
    for q in range(NX):
        b_copy(BWD - 1, q).wait_recv()
    for q in range(NX):
        f_copy(FWD - 1, q).wait_recv()

    def whole(q):
        return pair(z, q) + f_recv[FWD - 1, q].astype(f32) + b_recv[BWD - 1, q].astype(f32)

    x_copies = []
    for i, peer in enumerate(x_peers):
        x_send[i] = whole(lax.rem(x + i + 1, NX)).astype(bf16)
        copy = remote(x_send.at[i], x_recv.at[i], x_ss.at[i], x_rs.at[i], peer)
        copy.start()
        x_copies.append(copy)
    total = whole(x)
    for i in range(NX - 1):
        x_copies[i].wait_recv()
        total += x_recv[i].astype(f32)
    owned[...] = total

    for copy in x_copies + mp_copies:
        copy.wait_send()

    @pl.loop(0, NZ)
    def _(d):
        core_copy(d).wait_send()

    @pl.loop(0, FWD)
    def _(s):
        for q in range(NX):
            f_copy(s, q).wait_send()

            @pl.when(s < BWD)
            def _():
                b_copy(s, q).wait_send()


def reduce_all(outgoing, branch_parts, gn_parts):
    vmem = pl.BlockSpec(memory_space=pltpu.VMEM)
    dma = pltpu.SemaphoreType.DMA
    chunk = (NX, TOK, 128)
    feats = jax.ShapeDtypeStruct((TOK, 256), bf16)
    return pl.pallas_call(
        reduce_kernel,
        out_shape=(jax.ShapeDtypeStruct((TOK, 128), f32), feats, feats),
        in_specs=[vmem, vmem, vmem],
        out_specs=(vmem, vmem, vmem),
        scratch_shapes=[
            pltpu.VMEM((NZ,) + chunk, bf16),
            pltpu.VMEM((FWD,) + chunk, bf16),
            pltpu.VMEM((FWD,) + chunk, bf16),
            pltpu.VMEM((BWD,) + chunk, bf16),
            pltpu.VMEM((BWD,) + chunk, bf16),
            pltpu.VMEM((NX - 1, TOK, 128), bf16),
            pltpu.VMEM((NX - 1, TOK, 128), bf16),
            pltpu.VMEM((2, NMP - 1, TOK, 256), bf16),
            dma((NZ,)), dma((NZ,)),
            dma((FWD, NX)), dma((FWD, NX)),
            dma((BWD, NX)), dma((BWD, NX)),
            dma((NX - 1,)), dma((NX - 1,)),
            dma((2, NMP - 1)), dma((2, NMP - 1)),
        ],
        compiler_params=pltpu.CompilerParams(
            collective_id=1, has_side_effects=True, vmem_limit_bytes=16 << 20),
        name="reduce_all",
    )(outgoing.reshape(2, NZ, NX, TOK, 128), branch_parts, gn_parts)


def body(x_in, gain, w_in, w_out, grad_out, block_cols, slots):
    whole_x, whole_grad, weights = gather_inputs(x_in, grad_out, w_in, w_out)
    outgoing, branch_parts, gn_parts = compute(
        block_cols, slots, whole_x, whole_grad, gain.reshape(NMP, 1, 256), weights)
    owned, branch, grad_normed = reduce_all(outgoing, branch_parts, gn_parts)
    owned = owned.reshape(4, BLK // 2, 2, BLK).transpose(0, 2, 1, 3).reshape(1, 4, BLK * BLK)
    return (branch, grad_normed, owned)


def solution(mesh):
    placed = (
        P("dp", "mp"),
        P(),
        P("mp", None),
        P("mp", None),
        P("dp", "mp"),
        P("mp", None),
        P("mp", None),
    )
    return jax.shard_map(
        body,
        mesh=mesh,
        in_specs=placed,
        out_specs=(P("dp", "mp"), P("dp", "mp"), P("mp", "dp", None)),
        check_vma=False,
    )
```

```python
import functools
import math

import jax
import jax.numpy as jnp
from jax import lax
from jax.experimental import pallas as pl
from jax.experimental.pallas import tpu as pltpu
from jax.sharding import PartitionSpec as P

BLK = 64
NRB = 16
KR = 16
NCB = 128
TOK = 128
NX = 4
NZ = 16
NMP = 4
FWD = NZ // 2
BWD = NZ - 1 - FWD
RELAY_AT = 8
HALF = 64

norm_eps = 1e-06
tanh_coef = 0.7978845608028654
f32 = jnp.float32
bf16 = jnp.bfloat16
MESH = pl.DeviceIdType.MESH
NT = (((1,), (1,)), ((), ()))
TN = (((0,), (0,)), ((), ()))


def signal_all(peers):
    barrier = pltpu.get_barrier_semaphore()
    for peer in peers:
        pl.semaphore_signal(barrier, inc=1, device_id=peer, device_id_type=MESH)
    pl.semaphore_wait(barrier, len(peers))


def remote(src, dst, send, recv, peer):
    return pltpu.make_async_remote_copy(
        src_ref=src, dst_ref=dst, send_sem=send, recv_sem=recv,
        device_id=peer, device_id_type=MESH,
    )


def gather_kernel(x_ref, g_ref, wi_hbm, wo_hbm, xo_ref, go_ref, w_ref,
                  wi, wo, s_in, s_out, send, recv, load):
    me = lax.axis_index("mp")
    loads = [pltpu.make_async_copy(wi_hbm, wi, load.at[0]),
             pltpu.make_async_copy(wo_hbm, wo, load.at[1]),
             pltpu.make_async_copy(x_ref, xo_ref.at[me], load.at[2]),
             pltpu.make_async_copy(g_ref, go_ref.at[me], load.at[3])]
    for copy in loads:
        copy.start()
    nxt, prv = lax.rem(me + 1, NMP), lax.rem(me + NMP - 1, NMP)
    ahead, behind = {"mp": nxt}, {"mp": prv}
    signal_all([ahead, behind])
    x_ahead = remote(x_ref, xo_ref.at[me], send.at[0], recv.at[0], ahead)
    g_behind = remote(g_ref, go_ref.at[me], send.at[1], recv.at[1], behind)
    g_ahead = remote(g_ref, go_ref.at[me], send.at[2], recv.at[2], ahead)
    x_behind = remote(x_ref, xo_ref.at[me], send.at[3], recv.at[3], behind)
    x_relay = remote(xo_ref.at[prv], xo_ref.at[prv], send.at[4], recv.at[4], ahead)
    g_relay = remote(go_ref.at[nxt], go_ref.at[nxt], send.at[5], recv.at[5], behind)
    for copy in (x_ahead, g_behind, g_ahead, x_behind):
        copy.start()
    for copy in loads:
        copy.wait()
    low = lax.broadcasted_iota(jnp.int32, (8, 2 * BLK), 1) < BLK
    square = (2 * BLK, 2 * BLK)
    eye = (lax.broadcasted_iota(jnp.int32, square, 0)
           == lax.broadcasted_iota(jnp.int32, square, 1)).astype(f32).astype(bf16)

    def relayout(r):
        top = pl.ds(pl.multiple_of(r * KR, KR), KR)
        for j in range(BLK // 2):
            lanes = slice(j * 2 * BLK, (j + 1) * 2 * BLK)
            v = wi[top, lanes].astype(f32)
            a, b = v[:8], v[8:]
            for par, u in enumerate((jnp.where(low, a, pltpu.roll(b, BLK, 1)),
                                     jnp.where(low, pltpu.roll(a, BLK, 1), b))):
                group, row = divmod(2 * j + par, 8)
                s_in[pl.ds(group * BLK + row, 8, stride=8), :] = u
            v = wo[top, lanes].astype(f32)
            for h in range(2):
                for par, u in enumerate((pltpu.roll(v[h * 8:h * 8 + 8], BLK, 1), v[h * 8:h * 8 + 8])):
                    group, row = divmod(2 * j + par, 8)
                    s_out[pl.ds((h * 8 + group) * BLK + row, 8, stride=8), :] = u
        for k in range(8):
            block = jnp.concatenate(
                [s_in[g * BLK + k * 8:g * BLK + k * 8 + 8, :] for g in range(8)], axis=0)
            turned = lax.dot_general(eye, block.astype(bf16), NT, preferred_element_type=f32)
            for h in range(2):
                kk = h * 8 + k
                lower = jnp.concatenate([
                    s_out[(h * 8 + g) * BLK + k * 8:(h * 8 + g) * BLK + k * 8 + 8, BLK:]
                    for g in range(8)], axis=0)
                both = jnp.concatenate([turned[h * BLK:(h + 1) * BLK], lower], axis=1)
                w_ref[pl.ds(pl.multiple_of((r * KR + kk) * BLK, BLK), BLK), :] = both.astype(bf16)

    pl.loop(0, RELAY_AT)(relayout)
    x_ahead.wait_recv()
    x_relay.start()
    g_behind.wait_recv()
    g_relay.start()
    pl.loop(RELAY_AT, NRB)(relayout)
    for copy in (g_ahead, x_behind, x_relay, g_relay):
        copy.wait_recv()
    for copy in (x_ahead, g_behind, g_ahead, x_behind, x_relay, g_relay):
        copy.wait_send()


def gather_inputs(x_in, grad_out, w_in, w_out):
    whole = jax.ShapeDtypeStruct((NMP, TOK, x_in.shape[1]), bf16)
    vmem = pl.BlockSpec(memory_space=pltpu.VMEM)
    hbm = pl.BlockSpec(memory_space=pltpu.HBM)
    return pl.pallas_call(
        gather_kernel,
        out_shape=(whole, whole, jax.ShapeDtypeStruct((NRB * KR * BLK, 2 * BLK), bf16)),
        in_specs=[hbm, hbm, hbm, hbm],
        out_specs=(vmem, vmem, vmem),
        scratch_shapes=[
            pltpu.VMEM(w_in.shape, bf16),
            pltpu.VMEM(w_out.shape, bf16),
            pltpu.VMEM((KR * BLK // 2, 2 * BLK), f32),
            pltpu.VMEM((KR * BLK, 2 * BLK), f32),
            pltpu.SemaphoreType.DMA((6,)),
            pltpu.SemaphoreType.DMA((6,)),
            pltpu.SemaphoreType.DMA((4,)),
        ],
        compiler_params=pltpu.CompilerParams(
            collective_id=0, has_side_effects=True, vmem_limit_bytes=16 << 20),
        name="gather_inputs",
    )(*(pltpu.with_memory_space_constraint(a, pltpu.HBM) for a in (x_in, grad_out, w_in, w_out)))


def compute_kernel(scale, cols, slots, x_ref, g_ref, gain_ref, w_ref,
                   out_ref, branch_ref, gn_ref,
                   normed, pre, gact, act, gpre, parts, gath, halves, brt, gnt):
    squares = jnp.zeros((TOK, 1), f32)
    for p in range(NMP):
        xf = x_ref[p].astype(f32)
        squares += jnp.sum(xf * xf, axis=-1, keepdims=True)
    inv_rms = lax.rsqrt(squares / (NRB * BLK) + norm_eps)
    for p in range(NMP):
        normed[p] = (x_ref[p].astype(f32) * inv_rms * gain_ref[p]).astype(bf16)

    @pl.loop(0, NCB)
    def _(i):
        rows = pl.ds(pl.multiple_of(i * BLK, BLK), BLK)
        pre[rows, :] = jnp.zeros((BLK, TOK), f32)
        gact[rows, :] = jnp.zeros((BLK, TOK), f32)
        for j in range(4):
            out_ref[i * 4 + j] = jnp.zeros((BLK // 2, 2 * BLK), bf16)

    blank = jnp.zeros((TOK, BLK), bf16)

    def stacked(top, bottom):
        return jnp.concatenate([
            jnp.concatenate([top, blank], axis=1),
            jnp.concatenate([blank, bottom], axis=1),
        ], axis=0)

    @pl.loop(0, NMP)
    def _(p):
        for q in range(NRB // NMP):
            r = p * (NRB // NMP) + q
            lanes = slice(q * BLK, (q + 1) * BLK)
            both = stacked(normed[p, :, lanes], g_ref[p, :, lanes])
            rows = pl.ds(pl.multiple_of(r * KR * BLK, KR * BLK), KR * BLK)
            parts[...] = lax.dot_general(w_ref[rows, :], both, NT, preferred_element_type=f32)
            for k in range(KR):
                at = pl.ds(pl.multiple_of(cols[0, r * KR + k] * BLK, BLK), BLK)
                pre[at, :] += parts[k * BLK:(k + 1) * BLK, :TOK]
                gact[at, :] += parts[k * BLK:(k + 1) * BLK, TOK:]

    @pl.loop(0, NCB)
    def _(i):
        rows = pl.ds(pl.multiple_of(i * BLK, BLK), BLK)
        v = pre[rows, :]
        square = v * v
        th = jnp.tanh(tanh_coef * (v + 0.044715 * (square * v)))
        half = 0.5 * v
        act[rows, :] = (half * (1.0 + th)).astype(bf16)
        inner = tanh_coef * (1.0 + 0.134145 * square)
        slope = 0.5 * (1.0 + th) + half * (1.0 - th * th) * inner
        gpre[rows, :] = (gact[rows, :] * slope).astype(bf16)

    @pl.loop(0, NMP)
    def _(p):
        for q in range(NRB // NMP):
            r = p * (NRB // NMP) + q
            lanes = slice(q * BLK, (q + 1) * BLK)
            n_r = normed[p, :, lanes]
            for k in range(KR):
                at = pl.ds(pl.multiple_of(cols[0, r * KR + k] * BLK, BLK), BLK)
                block = gpre[at, :]
                gath[k * BLK:(k + 1) * BLK, :TOK] = block
                gath[k * BLK:(k + 1) * BLK, TOK:] = act[at, :]
                halves[k * 32:(k + 1) * 32, :TOK] = block[:32]
                halves[k * 32:(k + 1) * 32, TOK:] = block[32:]
            rows = pl.ds(pl.multiple_of(r * KR * BLK, KR * BLK), KR * BLK)
            sums = lax.dot_general(w_ref[rows, :], gath[...], TN, preferred_element_type=f32)
            at = pl.ds(pl.multiple_of(r * BLK, BLK), BLK)
            gnt[at, :] = sums[:BLK, :TOK]
            brt[at, :] = sums[BLK:, TOK:]
            grads = jnp.dot(halves[...], stacked(n_r, n_r), preferred_element_type=f32)
            grads = (grads * scale).astype(bf16)
            for k in range(KR):
                s = slots[0, r * KR + k]
                x, z, core, j = s // 128, (s // 8) % NZ, (s // 4) % 2, s % 4
                out_ref[((core * NZ + z) * NX + x) * 4 + j] = grads[k * 32:(k + 1) * 32]

    for p in range(NMP):
        rows = slice(p * 256, (p + 1) * 256)
        gn_ref[p] = gnt[rows, :].T.astype(bf16)
        branch_ref[p] = brt[rows, :].T.astype(bf16)


def compute(cols, slots, whole_x, whole_grad, gain, weights):
    vmem = pl.BlockSpec(memory_space=pltpu.VMEM)
    smem = pl.BlockSpec(memory_space=pltpu.SMEM)
    feats = jax.ShapeDtypeStruct((NMP, TOK, 256), bf16)
    scale = 1.0 / math.sqrt(TOK * 2 * NX * NZ)
    return pl.pallas_call(
        functools.partial(compute_kernel, scale),
        out_shape=(jax.ShapeDtypeStruct((512, BLK // 2, 2 * BLK), bf16), feats, feats),
        in_specs=[smem, smem, vmem, vmem, vmem, vmem],
        out_specs=(vmem, vmem, vmem),
        scratch_shapes=[
            pltpu.VMEM((NMP, TOK, 256), bf16),
            pltpu.VMEM((NCB * BLK, TOK), f32),
            pltpu.VMEM((NCB * BLK, TOK), f32),
            pltpu.VMEM((NCB * BLK, TOK), bf16),
            pltpu.VMEM((NCB * BLK, TOK), bf16),
            pltpu.VMEM((KR * BLK, 2 * TOK), f32),
            pltpu.VMEM((KR * BLK, 2 * TOK), bf16),
            pltpu.VMEM((KR * BLK // 2, 2 * TOK), bf16),
            pltpu.VMEM((NRB * BLK, TOK), f32),
            pltpu.VMEM((NRB * BLK, TOK), f32),
        ],
        compiler_params=pltpu.CompilerParams(vmem_limit_bytes=24 << 20),
        name="local_compute",
    )(cols, slots, whole_x, whole_grad, gain, weights)


def reduce_kernel(src, br_src, gn_src, owned, br_out, gn_out,
                  from_core, fa_send, fa_recv, ba_send, ba_recv, bx_send, bx_recv,
                  fb_send, fb_recv, bb_send, bb_recv, x_send, x_recv, m_recv,
                  core_ss, core_rs, fa_ss, fa_rs, ba_ss, ba_rs, bx_ss, bx_rs,
                  fb_ss, fb_rs, bb_ss, bb_rs, x_ss, x_rs, m_ss, m_rs):
    dp, mp = lax.axis_index("dp"), lax.axis_index("mp")
    core = lax.rem(dp, 2)
    z = lax.rem(dp // 2, NZ)
    x = dp // (2 * NZ)

    def at(xx, zz, cc):
        return {"dp": (xx * NZ + zz) * 2 + cc}

    partner = at(x, z, 1 - core)
    ahead = at(x, lax.rem(z + 1, NZ), core)
    behind = at(x, lax.rem(z + NZ - 1, NZ), core)
    x_peers = [at(lax.rem(x + i, NX), z, core) for i in range(1, NX)]
    m_peers = [{"mp": lax.rem(mp + i, NMP)} for i in range(1, NMP)]
    signal_all([partner, ahead, behind] + x_peers + m_peers)

    def f_dest(s):
        return lax.rem(z + FWD - s, NZ)

    def b_dest(s):
        return lax.rem(z + NZ - BWD + s, NZ)

    def core_copy(d):
        return remote(src.at[1 - core, d], from_core.at[d], core_ss.at[d], core_rs.at[d], partner)

    @pl.loop(0, FWD)
    def _(s):
        core_copy(f_dest(s)).start()
        core_copy(b_dest(s)).start()

    mp_copies = []
    for i, peer in enumerate(m_peers):
        to = lax.rem(mp + i + 1, NMP)
        mp_copies.append(remote(br_src.at[to], m_recv.at[0, i], m_ss.at[0, i], m_rs.at[0, i], peer))
        mp_copies.append(remote(gn_src.at[to], m_recv.at[1, i], m_ss.at[1, i], m_rs.at[1, i], peer))
    for copy in mp_copies:
        copy.start()

    def fa_copy(s, q):
        return remote(fa_send.at[s, q], fa_recv.at[s, q], fa_ss.at[s, q], fa_rs.at[s, q], ahead)

    def ba_copy(s, q):
        return remote(ba_send.at[s, q], ba_recv.at[s, q], ba_ss.at[s, q], ba_rs.at[s, q], behind)

    def bx_copy(s, i):
        return remote(bx_send.at[s, i], bx_recv.at[s, i], bx_ss.at[s, i], bx_rs.at[s, i], x_peers[i])

    def fb_copy(s):
        return remote(fb_send.at[s], fb_recv.at[s], fb_ss.at[s], fb_rs.at[s], ahead)

    def bb_copy(s):
        return remote(bb_send.at[s], bb_recv.at[s], bb_ss.at[s], bb_rs.at[s], behind)

    def upper(d, q):
        return src[core, d, q, :HALF].astype(f32) + from_core[d, q, :HALF].astype(f32)

    def lower(d, q):
        return src[core, d, q, HALF:].astype(f32) + from_core[d, q, HALF:].astype(f32)

    def a_step(s, first=False, back=True):
        for q in range(2):
            if not first:
                fa_copy(s - 1, q).wait_recv()
            for c in range(2):
                total = upper(f_dest(s), 2 * q + c)
                if not first:
                    total += fa_recv[s - 1, q, c].astype(f32)
                fa_send[s, q, c] = total.astype(bf16)
            fa_copy(s, q).start()
            if back:
                if not first:
                    ba_copy(s - 1, q).wait_recv()
                for c in range(2):
                    total = upper(b_dest(s), 2 * q + c)
                    if not first:
                        total += ba_recv[s - 1, q, c].astype(f32)
                    ba_send[s, q, c] = total.astype(bf16)
                ba_copy(s, q).start()

    def bx_step(s):
        core_copy(f_dest(s)).wait_recv()
        core_copy(b_dest(s)).wait_recv()
        for i in range(NX - 1):
            q = lax.rem(x + i + 1, NX)
            bx_send[s, i, 0] = lower(f_dest(s), q).astype(bf16)
            bx_send[s, i, 1] = lower(b_dest(s), q).astype(bf16)
            bx_copy(s, i).start()

    def row_sum(s, d, way):
        total = lower(d, x)
        for i in range(NX - 1):
            total += bx_recv[s, i, way].astype(f32)
        return total

    def bz_step(s, first=False, back=True):
        for i in range(NX - 1):
            bx_copy(s, i).wait_recv()
        total = row_sum(s, f_dest(s), 0)
        if not first:
            fb_copy(s - 1).wait_recv()
            total += fb_recv[s - 1].astype(f32)
        fb_send[s] = total.astype(bf16)
        fb_copy(s).start()
        if back:
            total = row_sum(s, b_dest(s), 1)
            if not first:
                bb_copy(s - 1).wait_recv()
                total += bb_recv[s - 1].astype(f32)
            bb_send[s] = total.astype(bf16)
            bb_copy(s).start()

    bx_step(0)
    a_step(0, first=True)
    bx_step(1)
    bz_step(0, first=True)

    @pl.loop(1, BWD)
    def _(s):
        a_step(s)
        bx_step(s + 1)
        bz_step(s)

    a_step(FWD - 1, back=False)
    bz_step(FWD - 1, back=False)

    for o, (out, own_part) in enumerate(((br_out, br_src), (gn_out, gn_src))):
        total = own_part[mp].astype(f32)
        for i in range(NMP - 1):
            mp_copies[2 * i + o].wait_recv()
            total += m_recv[o, i].astype(f32)
        out[...] = total.astype(bf16)

    for q in range(2):
        ba_copy(BWD - 1, q).wait_recv()
    for q in range(2):
        fa_copy(FWD - 1, q).wait_recv()

    def whole(q):
        return (upper(z, q) + fa_recv[FWD - 1, q // 2, lax.rem(q, 2)].astype(f32)
                + ba_recv[BWD - 1, q // 2, lax.rem(q, 2)].astype(f32))

    x_copies = []
    for i, peer in enumerate(x_peers):
        x_send[i] = whole(lax.rem(x + i + 1, NX)).astype(bf16)
        copy = remote(x_send.at[i], x_recv.at[i], x_ss.at[i], x_rs.at[i], peer)
        copy.start()
        x_copies.append(copy)

    bb_copy(BWD - 1).wait_recv()
    fb_copy(FWD - 1).wait_recv()
    owned[HALF:] = (row_sum(FWD - 1, z, 1) + fb_recv[FWD - 1].astype(f32)
                    + bb_recv[BWD - 1].astype(f32))
    total = whole(x)
    for i in range(NX - 1):
        x_copies[i].wait_recv()
        total += x_recv[i].astype(f32)
    owned[:HALF] = total

    for copy in x_copies + mp_copies:
        copy.wait_send()

    @pl.loop(0, NZ)
    def _(d):
        core_copy(d).wait_send()

    @pl.loop(0, FWD)
    def _(s):
        for q in range(2):
            fa_copy(s, q).wait_send()
        for i in range(NX - 1):
            bx_copy(s, i).wait_send()
        fb_copy(s).wait_send()

    @pl.loop(0, BWD)
    def _(s):
        for q in range(2):
            ba_copy(s, q).wait_send()
        bb_copy(s).wait_send()


def reduce_all(outgoing, branch_parts, gn_parts):
    vmem = pl.BlockSpec(memory_space=pltpu.VMEM)
    dma = pltpu.SemaphoreType.DMA
    part = (HALF, 2 * BLK)
    feats = jax.ShapeDtypeStruct((TOK, 256), bf16)

    def buf(*lead):
        return pltpu.VMEM(lead + part, bf16)

    return pl.pallas_call(
        reduce_kernel,
        out_shape=(jax.ShapeDtypeStruct((TOK, 128), f32), feats, feats),
        in_specs=[vmem, vmem, vmem],
        out_specs=(vmem, vmem, vmem),
        scratch_shapes=[
            pltpu.VMEM((NZ, NX, TOK, 128), bf16),
            buf(FWD, 2, 2), buf(FWD, 2, 2),
            buf(BWD, 2, 2), buf(BWD, 2, 2),
            buf(FWD, NX - 1, 2), buf(FWD, NX - 1, 2),
            buf(FWD), buf(FWD),
            buf(BWD), buf(BWD),
            buf(NX - 1), buf(NX - 1),
            pltpu.VMEM((2, NMP - 1, TOK, 256), bf16),
            dma((NZ,)), dma((NZ,)),
            dma((FWD, 2)), dma((FWD, 2)),
            dma((BWD, 2)), dma((BWD, 2)),
            dma((FWD, NX - 1)), dma((FWD, NX - 1)),
            dma((FWD,)), dma((FWD,)),
            dma((BWD,)), dma((BWD,)),
            dma((NX - 1,)), dma((NX - 1,)),
            dma((2, NMP - 1)), dma((2, NMP - 1)),
        ],
        compiler_params=pltpu.CompilerParams(
            collective_id=1, has_side_effects=True, vmem_limit_bytes=16 << 20),
        name="reduce_all",
    )(outgoing.reshape(2, NZ, NX, TOK, 128), branch_parts, gn_parts)


def body(x_in, gain, w_in, w_out, grad_out, block_cols, slots):
    whole_x, whole_grad, weights = gather_inputs(x_in, grad_out, w_in, w_out)
    outgoing, branch_parts, gn_parts = compute(
        block_cols, slots, whole_x, whole_grad, gain.reshape(NMP, 1, 256), weights)
    owned, branch, grad_normed = reduce_all(outgoing, branch_parts, gn_parts)
    owned = owned.reshape(4, BLK // 2, 2, BLK).transpose(0, 2, 1, 3).reshape(1, 4, BLK * BLK)
    return (branch, grad_normed, owned)


def solution(mesh):
    placed = (
        P("dp", "mp"),
        P(),
        P("mp", None),
        P("mp", None),
        P("dp", "mp"),
        P("mp", None),
        P("mp", None),
    )
    return jax.shard_map(
        body,
        mesh=mesh,
        in_specs=placed,
        out_specs=(P("dp", "mp"), P("dp", "mp"), P("mp", "dp", None)),
        check_vma=False,
    )
```

```python
import functools
import math

import jax
import jax.numpy as jnp
from jax import lax
from jax.experimental import pallas as pl
from jax.experimental.pallas import tpu as pltpu
from jax.sharding import PartitionSpec as P

BLK = 64
NRB = 16
KR = 16
NCB = 128
TOK = 128
NX = 4
NZ = 16
NMP = 4
FWD = NZ // 2
BWD = NZ - 1 - FWD
RELAY_AT = 8
HALF = 64

norm_eps = 1e-06
tanh_coef = 0.7978845608028654
f32 = jnp.float32
bf16 = jnp.bfloat16
MESH = pl.DeviceIdType.MESH
NT = (((1,), (1,)), ((), ()))
TN = (((0,), (0,)), ((), ()))


def signal_all(peers):
    barrier = pltpu.get_barrier_semaphore()
    for peer in peers:
        pl.semaphore_signal(barrier, inc=1, device_id=peer, device_id_type=MESH)
    pl.semaphore_wait(barrier, len(peers))


def remote(src, dst, send, recv, peer):
    return pltpu.make_async_remote_copy(
        src_ref=src, dst_ref=dst, send_sem=send, recv_sem=recv,
        device_id=peer, device_id_type=MESH,
    )


def gather_kernel(x_ref, g_ref, wi_hbm, wo_hbm, xo_ref, go_ref, w_ref,
                  wi, wo, s_in, s_out, send, recv, load):
    me = lax.axis_index("mp")
    loads = [pltpu.make_async_copy(wi_hbm, wi, load.at[0]),
             pltpu.make_async_copy(wo_hbm, wo, load.at[1]),
             pltpu.make_async_copy(x_ref, xo_ref.at[me], load.at[2]),
             pltpu.make_async_copy(g_ref, go_ref.at[me], load.at[3])]
    for copy in loads:
        copy.start()
    nxt, prv = lax.rem(me + 1, NMP), lax.rem(me + NMP - 1, NMP)
    ahead, behind = {"mp": nxt}, {"mp": prv}
    signal_all([ahead, behind])
    x_ahead = remote(x_ref, xo_ref.at[me], send.at[0], recv.at[0], ahead)
    g_behind = remote(g_ref, go_ref.at[me], send.at[1], recv.at[1], behind)
    g_ahead = remote(g_ref, go_ref.at[me], send.at[2], recv.at[2], ahead)
    x_behind = remote(x_ref, xo_ref.at[me], send.at[3], recv.at[3], behind)
    x_relay = remote(xo_ref.at[prv], xo_ref.at[prv], send.at[4], recv.at[4], ahead)
    g_relay = remote(go_ref.at[nxt], go_ref.at[nxt], send.at[5], recv.at[5], behind)
    for copy in (x_ahead, g_behind, g_ahead, x_behind):
        copy.start()
    for copy in loads:
        copy.wait()
    low = lax.broadcasted_iota(jnp.int32, (8, 2 * BLK), 1) < BLK
    square = (2 * BLK, 2 * BLK)
    eye = (lax.broadcasted_iota(jnp.int32, square, 0)
           == lax.broadcasted_iota(jnp.int32, square, 1)).astype(f32).astype(bf16)

    def relayout(r):
        top = pl.ds(pl.multiple_of(r * KR, KR), KR)
        for j in range(BLK // 2):
            lanes = slice(j * 2 * BLK, (j + 1) * 2 * BLK)
            v = wi[top, lanes].astype(f32)
            a, b = v[:8], v[8:]
            for par, u in enumerate((jnp.where(low, a, pltpu.roll(b, BLK, 1)),
                                     jnp.where(low, pltpu.roll(a, BLK, 1), b))):
                group, row = divmod(2 * j + par, 8)
                s_in[pl.ds(group * BLK + row, 8, stride=8), :] = u
            v = wo[top, lanes].astype(f32)
            for h in range(2):
                for par, u in enumerate((pltpu.roll(v[h * 8:h * 8 + 8], BLK, 1), v[h * 8:h * 8 + 8])):
                    group, row = divmod(2 * j + par, 8)
                    s_out[pl.ds((h * 8 + group) * BLK + row, 8, stride=8), :] = u
        for k in range(8):
            block = jnp.concatenate(
                [s_in[g * BLK + k * 8:g * BLK + k * 8 + 8, :] for g in range(8)], axis=0)
            turned = lax.dot_general(eye, block.astype(bf16), NT, preferred_element_type=f32)
            for h in range(2):
                kk = h * 8 + k
                lower = jnp.concatenate([
                    s_out[(h * 8 + g) * BLK + k * 8:(h * 8 + g) * BLK + k * 8 + 8, BLK:]
                    for g in range(8)], axis=0)
                both = jnp.concatenate([turned[h * BLK:(h + 1) * BLK], lower], axis=1)
                w_ref[pl.ds(pl.multiple_of((r * KR + kk) * BLK, BLK), BLK), :] = both.astype(bf16)

    pl.loop(0, RELAY_AT)(relayout)
    x_ahead.wait_recv()
    x_relay.start()
    g_behind.wait_recv()
    g_relay.start()
    pl.loop(RELAY_AT, NRB)(relayout)
    for copy in (g_ahead, x_behind, x_relay, g_relay):
        copy.wait_recv()
    for copy in (x_ahead, g_behind, g_ahead, x_behind, x_relay, g_relay):
        copy.wait_send()


def gather_inputs(x_in, grad_out, w_in, w_out):
    whole = jax.ShapeDtypeStruct((NMP, TOK, x_in.shape[1]), bf16)
    vmem = pl.BlockSpec(memory_space=pltpu.VMEM)
    hbm = pl.BlockSpec(memory_space=pltpu.HBM)
    return pl.pallas_call(
        gather_kernel,
        out_shape=(whole, whole, jax.ShapeDtypeStruct((NRB * KR * BLK, 2 * BLK), bf16)),
        in_specs=[hbm, hbm, hbm, hbm],
        out_specs=(vmem, vmem, vmem),
        scratch_shapes=[
            pltpu.VMEM(w_in.shape, bf16),
            pltpu.VMEM(w_out.shape, bf16),
            pltpu.VMEM((KR * BLK // 2, 2 * BLK), f32),
            pltpu.VMEM((KR * BLK, 2 * BLK), f32),
            pltpu.SemaphoreType.DMA((6,)),
            pltpu.SemaphoreType.DMA((6,)),
            pltpu.SemaphoreType.DMA((4,)),
        ],
        compiler_params=pltpu.CompilerParams(
            collective_id=0, has_side_effects=True, vmem_limit_bytes=16 << 20),
        name="gather_inputs",
    )(*(pltpu.with_memory_space_constraint(a, pltpu.HBM) for a in (x_in, grad_out, w_in, w_out)))


def compute_kernel(scale, cols, slots, x_ref, g_ref, gain_ref, w_ref,
                   out_ref, branch_ref, gn_ref,
                   normed, pre, gact, act, gpre, brt, gnt):
    squares = jnp.zeros((TOK, 1), f32)
    for p in range(NMP):
        xf = x_ref[p].astype(f32)
        squares += jnp.sum(xf * xf, axis=-1, keepdims=True)
    inv_rms = lax.rsqrt(squares / (NRB * BLK) + norm_eps)
    for p in range(NMP):
        normed[p] = (x_ref[p].astype(f32) * inv_rms * gain_ref[p]).astype(bf16)

    @pl.loop(0, NCB)
    def _(i):
        rows = pl.ds(pl.multiple_of(i * BLK, BLK), BLK)
        pre[rows, :] = jnp.zeros((BLK, TOK), f32)
        gact[rows, :] = jnp.zeros((BLK, TOK), f32)
        for j in range(4):
            out_ref[i * 4 + j] = jnp.zeros((BLK // 2, 2 * BLK), bf16)

    blank = jnp.zeros((TOK, BLK), bf16)

    def stacked(top, bottom):
        return jnp.concatenate([
            jnp.concatenate([top, blank], axis=1),
            jnp.concatenate([blank, bottom], axis=1),
        ], axis=0)

    @pl.loop(0, NMP)
    def _(p):
        for q in range(NRB // NMP):
            r = p * (NRB // NMP) + q
            lanes = slice(q * BLK, (q + 1) * BLK)
            both = stacked(normed[p, :, lanes], g_ref[p, :, lanes])
            rows = pl.ds(pl.multiple_of(r * KR * BLK, KR * BLK), KR * BLK)
            parts = lax.dot_general(w_ref[rows, :], both, NT, preferred_element_type=f32)
            for k in range(KR):
                at = pl.ds(pl.multiple_of(cols[0, r * KR + k] * BLK, BLK), BLK)
                pre[at, :] += parts[k * BLK:(k + 1) * BLK, :TOK]
                gact[at, :] += parts[k * BLK:(k + 1) * BLK, TOK:]

    @pl.loop(0, NCB // 4)
    def _(i):
        rows = pl.ds(pl.multiple_of(i * (4 * BLK), 4 * BLK), 4 * BLK)
        v = pre[rows, :]
        square = v * v
        th = jnp.tanh(v * (tanh_coef + (tanh_coef * 0.044715) * square))
        rise = 0.5 + 0.5 * th
        value = v * rise
        act[rows, :] = value.astype(bf16)
        inner = tanh_coef + (tanh_coef * 0.134145) * square
        slope = rise + value * (1.0 - th) * inner
        gpre[rows, :] = (gact[rows, :] * slope).astype(bf16)

    @pl.loop(0, NMP)
    def _(p):
        for q in range(NRB // NMP):
            r = p * (NRB // NMP) + q
            lanes = slice(q * BLK, (q + 1) * BLK)
            n_r = normed[p, :, lanes]
            ats = [pl.ds(pl.multiple_of(cols[0, r * KR + k] * BLK, BLK), BLK) for k in range(KR)]
            gath = jnp.concatenate(
                [jnp.concatenate([gpre[at, :], act[at, :]], axis=1) for at in ats], axis=0)
            halves = jnp.concatenate([
                jnp.concatenate([gpre[at, :][:32], gpre[at, :][32:]], axis=1) for at in ats], axis=0)
            rows = pl.ds(pl.multiple_of(r * KR * BLK, KR * BLK), KR * BLK)
            sums = lax.dot_general(w_ref[rows, :], gath, TN, preferred_element_type=f32)
            at = pl.ds(pl.multiple_of(r * BLK, BLK), BLK)
            gnt[at, :] = sums[:BLK, :TOK]
            brt[at, :] = sums[BLK:, TOK:]
            grads = jnp.dot(halves, stacked(n_r, n_r), preferred_element_type=f32)
            grads = (grads * scale).astype(bf16)
            for k in range(KR):
                s = slots[0, r * KR + k]
                x, z, core, j = s // 128, (s // 8) % NZ, (s // 4) % 2, s % 4
                out_ref[((core * NZ + z) * NX + x) * 4 + j] = grads[k * 32:(k + 1) * 32]

    for p in range(NMP):
        rows = slice(p * 256, (p + 1) * 256)
        gn_ref[p] = gnt[rows, :].T.astype(bf16)
        branch_ref[p] = brt[rows, :].T.astype(bf16)


def compute(cols, slots, whole_x, whole_grad, gain, weights):
    vmem = pl.BlockSpec(memory_space=pltpu.VMEM)
    smem = pl.BlockSpec(memory_space=pltpu.SMEM)
    feats = jax.ShapeDtypeStruct((NMP, TOK, 256), bf16)
    scale = 1.0 / math.sqrt(TOK * 2 * NX * NZ)
    return pl.pallas_call(
        functools.partial(compute_kernel, scale),
        out_shape=(jax.ShapeDtypeStruct((512, BLK // 2, 2 * BLK), bf16), feats, feats),
        in_specs=[smem, smem, vmem, vmem, vmem, vmem],
        out_specs=(vmem, vmem, vmem),
        scratch_shapes=[
            pltpu.VMEM((NMP, TOK, 256), bf16),
            pltpu.VMEM((NCB * BLK, TOK), f32),
            pltpu.VMEM((NCB * BLK, TOK), f32),
            pltpu.VMEM((NCB * BLK, TOK), bf16),
            pltpu.VMEM((NCB * BLK, TOK), bf16),
            pltpu.VMEM((NRB * BLK, TOK), f32),
            pltpu.VMEM((NRB * BLK, TOK), f32),
        ],
        compiler_params=pltpu.CompilerParams(vmem_limit_bytes=24 << 20),
        name="local_compute",
    )(cols, slots, whole_x, whole_grad, gain, weights)


def reduce_kernel(src, br_src, gn_src, owned, br_out, gn_out,
                  from_core, fa_send, fa_recv, ba_send, ba_recv, bx_send, bx_recv,
                  fb_send, fb_recv, bb_send, bb_recv, x_send, x_recv, m_recv,
                  core_ss, core_rs, fa_ss, fa_rs, ba_ss, ba_rs, bx_ss, bx_rs,
                  fb_ss, fb_rs, bb_ss, bb_rs, x_ss, x_rs, m_ss, m_rs):
    dp, mp = lax.axis_index("dp"), lax.axis_index("mp")
    core = lax.rem(dp, 2)
    z = lax.rem(dp // 2, NZ)
    x = dp // (2 * NZ)

    def at(xx, zz, cc):
        return {"dp": (xx * NZ + zz) * 2 + cc}

    partner = at(x, z, 1 - core)
    ahead = at(x, lax.rem(z + 1, NZ), core)
    behind = at(x, lax.rem(z + NZ - 1, NZ), core)
    x_peers = [at(lax.rem(x + i, NX), z, core) for i in range(1, NX)]
    m_peers = [{"mp": lax.rem(mp + i, NMP)} for i in range(1, NMP)]
    signal_all([partner, ahead, behind] + x_peers + m_peers)

    def f_dest(s):
        return lax.rem(z + FWD - s, NZ)

    def b_dest(s):
        return lax.rem(z + NZ - BWD + s, NZ)

    def core_copy(d):
        return remote(src.at[1 - core, d], from_core.at[d], core_ss.at[d], core_rs.at[d], partner)

    @pl.loop(0, FWD)
    def _(s):
        core_copy(f_dest(s)).start()
        core_copy(b_dest(s)).start()

    mp_copies = []
    for i, peer in enumerate(m_peers):
        to = lax.rem(mp + i + 1, NMP)
        mp_copies.append(remote(br_src.at[to], m_recv.at[0, i], m_ss.at[0, i], m_rs.at[0, i], peer))
        mp_copies.append(remote(gn_src.at[to], m_recv.at[1, i], m_ss.at[1, i], m_rs.at[1, i], peer))
    for copy in mp_copies:
        copy.start()

    def fa_copy(s, q):
        return remote(fa_send.at[s, q], fa_recv.at[s, q], fa_ss.at[s, q], fa_rs.at[s, q], ahead)

    def ba_copy(s, q):
        return remote(ba_send.at[s, q], ba_recv.at[s, q], ba_ss.at[s, q], ba_rs.at[s, q], behind)

    def bx_copy(s, i):
        return remote(bx_send.at[s, i], bx_recv.at[s, i], bx_ss.at[s, i], bx_rs.at[s, i], x_peers[i])

    def fb_copy(s):
        return remote(fb_send.at[s], fb_recv.at[s], fb_ss.at[s], fb_rs.at[s], ahead)

    def bb_copy(s):
        return remote(bb_send.at[s], bb_recv.at[s], bb_ss.at[s], bb_rs.at[s], behind)

    def upper(d, q):
        return src[core, d, q, :HALF].astype(f32) + from_core[d, q, :HALF].astype(f32)

    def lower(d, q):
        return src[core, d, q, HALF:].astype(f32) + from_core[d, q, HALF:].astype(f32)

    def a_step(s, first=False, back=True):
        for q in range(NX):
            total = upper(f_dest(s), q)
            if not first:
                fa_copy(s - 1, q).wait_recv()
                total += fa_recv[s - 1, q].astype(f32)
            fa_send[s, q] = total.astype(bf16)
            fa_copy(s, q).start()
            if back:
                total = upper(b_dest(s), q)
                if not first:
                    ba_copy(s - 1, q).wait_recv()
                    total += ba_recv[s - 1, q].astype(f32)
                ba_send[s, q] = total.astype(bf16)
                ba_copy(s, q).start()

    def bx_step(s):
        core_copy(f_dest(s)).wait_recv()
        core_copy(b_dest(s)).wait_recv()
        for i in range(NX - 1):
            q = lax.rem(x + i + 1, NX)
            bx_send[s, i, 0] = lower(f_dest(s), q).astype(bf16)
            bx_send[s, i, 1] = lower(b_dest(s), q).astype(bf16)
            bx_copy(s, i).start()

    def row_sum(s, d, way):
        total = lower(d, x)
        for i in range(NX - 1):
            total += bx_recv[s, i, way].astype(f32)
        return total

    def bz_step(s, first=False, back=True):
        for i in range(NX - 1):
            bx_copy(s, i).wait_recv()
        total = row_sum(s, f_dest(s), 0)
        if not first:
            fb_copy(s - 1).wait_recv()
            total += fb_recv[s - 1].astype(f32)
        fb_send[s] = total.astype(bf16)
        fb_copy(s).start()
        if back:
            total = row_sum(s, b_dest(s), 1)
            if not first:
                bb_copy(s - 1).wait_recv()
                total += bb_recv[s - 1].astype(f32)
            bb_send[s] = total.astype(bf16)
            bb_copy(s).start()

    bx_step(0)
    a_step(0, first=True)
    bx_step(1)
    bz_step(0, first=True)
    a_step(1)
    bx_step(2)

    @pl.loop(2, BWD)
    def _(s):
        bz_step(s - 1)
        a_step(s)
        bx_step(s + 1)

    bz_step(BWD - 1)
    a_step(FWD - 1, back=False)
    bz_step(FWD - 1, back=False)

    for o, (out, own_part) in enumerate(((br_out, br_src), (gn_out, gn_src))):
        total = own_part[mp].astype(f32)
        for i in range(NMP - 1):
            mp_copies[2 * i + o].wait_recv()
            total += m_recv[o, i].astype(f32)
        out[...] = total.astype(bf16)

    for q in range(NX):
        ba_copy(BWD - 1, q).wait_recv()
    for q in range(NX):
        fa_copy(FWD - 1, q).wait_recv()

    def whole(q):
        return (upper(z, q) + fa_recv[FWD - 1, q].astype(f32)
                + ba_recv[BWD - 1, q].astype(f32))

    x_copies = []
    for i, peer in enumerate(x_peers):
        x_send[i] = whole(lax.rem(x + i + 1, NX)).astype(bf16)
        copy = remote(x_send.at[i], x_recv.at[i], x_ss.at[i], x_rs.at[i], peer)
        copy.start()
        x_copies.append(copy)

    bb_copy(BWD - 1).wait_recv()
    fb_copy(FWD - 1).wait_recv()
    owned[HALF:] = (row_sum(FWD - 1, z, 1) + fb_recv[FWD - 1].astype(f32)
                    + bb_recv[BWD - 1].astype(f32))
    total = whole(x)
    for i in range(NX - 1):
        x_copies[i].wait_recv()
        total += x_recv[i].astype(f32)
    owned[:HALF] = total

    for copy in x_copies + mp_copies:
        copy.wait_send()

    @pl.loop(0, NZ)
    def _(d):
        core_copy(d).wait_send()

    @pl.loop(0, FWD)
    def _(s):
        for q in range(NX):
            fa_copy(s, q).wait_send()
        for i in range(NX - 1):
            bx_copy(s, i).wait_send()
        fb_copy(s).wait_send()

    @pl.loop(0, BWD)
    def _(s):
        for q in range(NX):
            ba_copy(s, q).wait_send()
        bb_copy(s).wait_send()


def reduce_all(outgoing, branch_parts, gn_parts):
    vmem = pl.BlockSpec(memory_space=pltpu.VMEM)
    dma = pltpu.SemaphoreType.DMA
    part = (HALF, 2 * BLK)
    feats = jax.ShapeDtypeStruct((TOK, 256), bf16)

    def buf(*lead):
        return pltpu.VMEM(lead + part, bf16)

    return pl.pallas_call(
        reduce_kernel,
        out_shape=(jax.ShapeDtypeStruct((TOK, 128), f32), feats, feats),
        in_specs=[vmem, vmem, vmem],
        out_specs=(vmem, vmem, vmem),
        scratch_shapes=[
            pltpu.VMEM((NZ, NX, TOK, 128), bf16),
            buf(FWD, NX), buf(FWD, NX),
            buf(BWD, NX), buf(BWD, NX),
            buf(FWD, NX - 1, 2), buf(FWD, NX - 1, 2),
            buf(FWD), buf(FWD),
            buf(BWD), buf(BWD),
            buf(NX - 1), buf(NX - 1),
            pltpu.VMEM((2, NMP - 1, TOK, 256), bf16),
            dma((NZ,)), dma((NZ,)),
            dma((FWD, NX)), dma((FWD, NX)),
            dma((BWD, NX)), dma((BWD, NX)),
            dma((FWD, NX - 1)), dma((FWD, NX - 1)),
            dma((FWD,)), dma((FWD,)),
            dma((BWD,)), dma((BWD,)),
            dma((NX - 1,)), dma((NX - 1,)),
            dma((2, NMP - 1)), dma((2, NMP - 1)),
        ],
        compiler_params=pltpu.CompilerParams(
            collective_id=1, has_side_effects=True, vmem_limit_bytes=16 << 20),
        name="reduce_all",
    )(outgoing.reshape(2, NZ, NX, TOK, 128), branch_parts, gn_parts)


def body(x_in, gain, w_in, w_out, grad_out, block_cols, slots):
    whole_x, whole_grad, weights = gather_inputs(x_in, grad_out, w_in, w_out)
    outgoing, branch_parts, gn_parts = compute(
        block_cols, slots, whole_x, whole_grad, gain.reshape(NMP, 1, 256), weights)
    owned, branch, grad_normed = reduce_all(outgoing, branch_parts, gn_parts)
    owned = owned.reshape(4, BLK // 2, 2, BLK).transpose(0, 2, 1, 3).reshape(1, 4, BLK * BLK)
    return (branch, grad_normed, owned)


def solution(mesh):
    placed = (
        P("dp", "mp"),
        P(),
        P("mp", None),
        P("mp", None),
        P("dp", "mp"),
        P("mp", None),
        P("mp", None),
    )
    return jax.shard_map(
        body,
        mesh=mesh,
        in_specs=placed,
        out_specs=(P("dp", "mp"), P("dp", "mp"), P("mp", "dp", None)),
        check_vma=False,
    )
```

```python
import functools
import math

import jax
import jax.numpy as jnp
from jax import lax
from jax.experimental import pallas as pl
from jax.experimental.pallas import tpu as pltpu
from jax.sharding import PartitionSpec as P

BLK = 64
NRB = 16
KR = 16
NCB = 128
TOK = 128
NX = 4
NZ = 16
NMP = 4
FWD = NZ // 2
BWD = NZ - 1 - FWD
RELAY_AT = 8
HALF = 64

norm_eps = 1e-06
tanh_coef = 0.7978845608028654
f32 = jnp.float32
bf16 = jnp.bfloat16
MESH = pl.DeviceIdType.MESH
NT = (((1,), (1,)), ((), ()))
TN = (((0,), (0,)), ((), ()))


def signal_all(peers):
    barrier = pltpu.get_barrier_semaphore()
    for peer in peers:
        pl.semaphore_signal(barrier, inc=1, device_id=peer, device_id_type=MESH)
    pl.semaphore_wait(barrier, len(peers))


def remote(src, dst, send, recv, peer):
    return pltpu.make_async_remote_copy(
        src_ref=src, dst_ref=dst, send_sem=send, recv_sem=recv,
        device_id=peer, device_id_type=MESH,
    )


def gather_kernel(x_ref, g_ref, wi_hbm, wo_hbm, xo_ref, go_ref, w_ref,
                  wi, wo, s_in, s_out, send, recv, load):
    me = lax.axis_index("mp")
    loads = [pltpu.make_async_copy(wi_hbm, wi, load.at[0]),
             pltpu.make_async_copy(wo_hbm, wo, load.at[1]),
             pltpu.make_async_copy(x_ref, xo_ref.at[me], load.at[2]),
             pltpu.make_async_copy(g_ref, go_ref.at[me], load.at[3])]
    for copy in loads:
        copy.start()
    nxt, prv = lax.rem(me + 1, NMP), lax.rem(me + NMP - 1, NMP)
    ahead, behind = {"mp": nxt}, {"mp": prv}
    signal_all([ahead, behind])
    x_ahead = remote(x_ref, xo_ref.at[me], send.at[0], recv.at[0], ahead)
    g_behind = remote(g_ref, go_ref.at[me], send.at[1], recv.at[1], behind)
    g_ahead = remote(g_ref, go_ref.at[me], send.at[2], recv.at[2], ahead)
    x_behind = remote(x_ref, xo_ref.at[me], send.at[3], recv.at[3], behind)
    x_relay = remote(xo_ref.at[prv], xo_ref.at[prv], send.at[4], recv.at[4], ahead)
    g_relay = remote(go_ref.at[nxt], go_ref.at[nxt], send.at[5], recv.at[5], behind)
    for copy in (x_ahead, g_behind, g_ahead, x_behind):
        copy.start()
    for copy in loads:
        copy.wait()
    low = lax.broadcasted_iota(jnp.int32, (8, 2 * BLK), 1) < BLK
    square = (2 * BLK, 2 * BLK)
    eye = (lax.broadcasted_iota(jnp.int32, square, 0)
           == lax.broadcasted_iota(jnp.int32, square, 1)).astype(f32).astype(bf16)

    def relayout(r):
        top = pl.ds(pl.multiple_of(r * KR, KR), KR)
        for j in range(BLK // 2):
            lanes = slice(j * 2 * BLK, (j + 1) * 2 * BLK)
            v = wi[top, lanes].astype(f32)
            a, b = v[:8], v[8:]
            for par, u in enumerate((jnp.where(low, a, pltpu.roll(b, BLK, 1)),
                                     jnp.where(low, pltpu.roll(a, BLK, 1), b))):
                group, row = divmod(2 * j + par, 8)
                s_in[pl.ds(group * BLK + row, 8, stride=8), :] = u
            v = wo[top, lanes].astype(f32)
            for h in range(2):
                for par, u in enumerate((pltpu.roll(v[h * 8:h * 8 + 8], BLK, 1), v[h * 8:h * 8 + 8])):
                    group, row = divmod(2 * j + par, 8)
                    s_out[pl.ds((h * 8 + group) * BLK + row, 8, stride=8), :] = u
        for k in range(8):
            block = jnp.concatenate(
                [s_in[g * BLK + k * 8:g * BLK + k * 8 + 8, :] for g in range(8)], axis=0)
            turned = lax.dot_general(eye, block.astype(bf16), NT, preferred_element_type=f32)
            for h in range(2):
                kk = h * 8 + k
                lower = jnp.concatenate([
                    s_out[(h * 8 + g) * BLK + k * 8:(h * 8 + g) * BLK + k * 8 + 8, BLK:]
                    for g in range(8)], axis=0)
                both = jnp.concatenate([turned[h * BLK:(h + 1) * BLK], lower], axis=1)
                w_ref[pl.ds(pl.multiple_of((r * KR + kk) * BLK, BLK), BLK), :] = both.astype(bf16)

    pl.loop(0, RELAY_AT)(relayout)
    x_ahead.wait_recv()
    x_relay.start()
    g_behind.wait_recv()
    g_relay.start()
    pl.loop(RELAY_AT, NRB)(relayout)
    for copy in (g_ahead, x_behind, x_relay, g_relay):
        copy.wait_recv()
    for copy in (x_ahead, g_behind, g_ahead, x_behind, x_relay, g_relay):
        copy.wait_send()


def gather_inputs(x_in, grad_out, w_in, w_out):
    whole = jax.ShapeDtypeStruct((NMP, TOK, x_in.shape[1]), bf16)
    vmem = pl.BlockSpec(memory_space=pltpu.VMEM)
    hbm = pl.BlockSpec(memory_space=pltpu.HBM)
    return pl.pallas_call(
        gather_kernel,
        out_shape=(whole, whole, jax.ShapeDtypeStruct((NRB * KR * BLK, 2 * BLK), bf16)),
        in_specs=[hbm, hbm, hbm, hbm],
        out_specs=(vmem, vmem, vmem),
        scratch_shapes=[
            pltpu.VMEM(w_in.shape, bf16),
            pltpu.VMEM(w_out.shape, bf16),
            pltpu.VMEM((KR * BLK // 2, 2 * BLK), f32),
            pltpu.VMEM((KR * BLK, 2 * BLK), f32),
            pltpu.SemaphoreType.DMA((6,)),
            pltpu.SemaphoreType.DMA((6,)),
            pltpu.SemaphoreType.DMA((4,)),
        ],
        compiler_params=pltpu.CompilerParams(
            collective_id=0, has_side_effects=True, vmem_limit_bytes=16 << 20),
        name="gather_inputs",
    )(*(pltpu.with_memory_space_constraint(a, pltpu.HBM) for a in (x_in, grad_out, w_in, w_out)))


def compute_kernel(scale, cols, slots, x_ref, g_ref, gain_ref, w_ref,
                   out_ref, branch_ref, gn_ref,
                   normed, pre, gact, act, gpre, brt, gnt):
    squares = jnp.zeros((TOK, 1), f32)
    for p in range(NMP):
        xf = x_ref[p].astype(f32)
        squares += jnp.sum(xf * xf, axis=-1, keepdims=True)
    inv_rms = lax.rsqrt(squares / (NRB * BLK) + norm_eps)
    for p in range(NMP):
        normed[p] = (x_ref[p].astype(f32) * inv_rms * gain_ref[p]).astype(bf16)

    @pl.loop(0, NCB)
    def _(i):
        rows = pl.ds(pl.multiple_of(i * BLK, BLK), BLK)
        pre[rows, :] = jnp.zeros((BLK, TOK), f32)
        gact[rows, :] = jnp.zeros((BLK, TOK), f32)
        for j in range(4):
            out_ref[i * 4 + j] = jnp.zeros((BLK // 2, 2 * BLK), bf16)

    blank = jnp.zeros((TOK, BLK), bf16)

    def stacked(top, bottom):
        return jnp.concatenate([
            jnp.concatenate([top, blank], axis=1),
            jnp.concatenate([blank, bottom], axis=1),
        ], axis=0)

    @pl.loop(0, NMP)
    def _(p):
        for q in range(NRB // NMP):
            r = p * (NRB // NMP) + q
            lanes = slice(q * BLK, (q + 1) * BLK)
            both = stacked(normed[p, :, lanes], g_ref[p, :, lanes])
            rows = pl.ds(pl.multiple_of(r * KR * BLK, KR * BLK), KR * BLK)
            parts = lax.dot_general(w_ref[rows, :], both, NT, preferred_element_type=f32)
            for k in range(KR):
                at = pl.ds(pl.multiple_of(cols[0, r * KR + k] * BLK, BLK), BLK)
                pre[at, :] += parts[k * BLK:(k + 1) * BLK, :TOK]
                gact[at, :] += parts[k * BLK:(k + 1) * BLK, TOK:]

    @pl.loop(0, NCB // 4)
    def _(i):
        rows = pl.ds(pl.multiple_of(i * (4 * BLK), 4 * BLK), 4 * BLK)
        v = pre[rows, :]
        square = v * v
        th = jnp.tanh(v * (tanh_coef + (tanh_coef * 0.044715) * square))
        rise = 0.5 + 0.5 * th
        value = v * rise
        act[rows, :] = value.astype(bf16)
        inner = tanh_coef + (tanh_coef * 0.134145) * square
        slope = rise + value * (1.0 - th) * inner
        gpre[rows, :] = (gact[rows, :] * slope).astype(bf16)

    @pl.loop(0, NMP)
    def _(p):
        for q in range(NRB // NMP):
            r = p * (NRB // NMP) + q
            lanes = slice(q * BLK, (q + 1) * BLK)
            n_r = normed[p, :, lanes]
            ats = [pl.ds(pl.multiple_of(cols[0, r * KR + k] * BLK, BLK), BLK) for k in range(KR)]
            gath = jnp.concatenate(
                [jnp.concatenate([gpre[at, :], act[at, :]], axis=1) for at in ats], axis=0)
            halves = jnp.concatenate([
                jnp.concatenate([gpre[at, :][:32], gpre[at, :][32:]], axis=1) for at in ats], axis=0)
            rows = pl.ds(pl.multiple_of(r * KR * BLK, KR * BLK), KR * BLK)
            sums = lax.dot_general(w_ref[rows, :], gath, TN, preferred_element_type=f32)
            at = pl.ds(pl.multiple_of(r * BLK, BLK), BLK)
            gnt[at, :] = sums[:BLK, :TOK]
            brt[at, :] = sums[BLK:, TOK:]
            grads = jnp.dot(halves, stacked(n_r, n_r), preferred_element_type=f32)
            grads = (grads * scale).astype(bf16)
            for k in range(KR):
                s = slots[0, r * KR + k]
                x, z, core, j = s // 128, (s // 8) % NZ, (s // 4) % 2, s % 4
                out_ref[((core * NZ + z) * NX + x) * 4 + j] = grads[k * 32:(k + 1) * 32]

    for p in range(NMP):
        rows = slice(p * 256, (p + 1) * 256)
        gn_ref[p] = gnt[rows, :].T.astype(bf16)
        branch_ref[p] = brt[rows, :].T.astype(bf16)


def compute(cols, slots, whole_x, whole_grad, gain, weights):
    vmem = pl.BlockSpec(memory_space=pltpu.VMEM)
    smem = pl.BlockSpec(memory_space=pltpu.SMEM)
    feats = jax.ShapeDtypeStruct((NMP, TOK, 256), bf16)
    scale = 1.0 / math.sqrt(TOK * 2 * NX * NZ)
    return pl.pallas_call(
        functools.partial(compute_kernel, scale),
        out_shape=(jax.ShapeDtypeStruct((512, BLK // 2, 2 * BLK), bf16), feats, feats),
        in_specs=[smem, smem, vmem, vmem, vmem, vmem],
        out_specs=(vmem, vmem, vmem),
        scratch_shapes=[
            pltpu.VMEM((NMP, TOK, 256), bf16),
            pltpu.VMEM((NCB * BLK, TOK), f32),
            pltpu.VMEM((NCB * BLK, TOK), f32),
            pltpu.VMEM((NCB * BLK, TOK), bf16),
            pltpu.VMEM((NCB * BLK, TOK), bf16),
            pltpu.VMEM((NRB * BLK, TOK), f32),
            pltpu.VMEM((NRB * BLK, TOK), f32),
        ],
        compiler_params=pltpu.CompilerParams(vmem_limit_bytes=24 << 20),
        name="local_compute",
    )(cols, slots, whole_x, whole_grad, gain, weights)


def reduce_kernel(src, br_src, gn_src, owned, br_out, gn_out,
                  from_core, fa_send, fa_recv, ba_send, ba_recv, bx_send, bx_recv,
                  fb_send, fb_recv, bb_send, bb_recv, x_send, x_recv, m_recv,
                  core_ss, core_rs, fa_ss, fa_rs, ba_ss, ba_rs, bx_ss, bx_rs,
                  fb_ss, fb_rs, bb_ss, bb_rs, x_ss, x_rs, m_ss, m_rs):
    dp, mp = lax.axis_index("dp"), lax.axis_index("mp")
    core = lax.rem(dp, 2)
    z = lax.rem(dp // 2, NZ)
    x = dp // (2 * NZ)

    def at(xx, zz, cc):
        return {"dp": (xx * NZ + zz) * 2 + cc}

    partner = at(x, z, 1 - core)
    ahead = at(x, lax.rem(z + 1, NZ), core)
    behind = at(x, lax.rem(z + NZ - 1, NZ), core)
    x_peers = [at(lax.rem(x + i, NX), z, core) for i in range(1, NX)]
    m_peers = [{"mp": lax.rem(mp + i, NMP)} for i in range(1, NMP)]
    signal_all([partner, ahead, behind] + x_peers + m_peers)

    def f_dest(s):
        return lax.rem(z + FWD - s, NZ)

    def b_dest(s):
        return lax.rem(z + NZ - BWD + s, NZ)

    def core_copy(d):
        return remote(src.at[1 - core, d], from_core.at[d], core_ss.at[d], core_rs.at[d], partner)

    def core_start(s):
        core_copy(f_dest(s)).start()
        core_copy(b_dest(s)).start()

    def m_copy(o, i):
        to = lax.rem(mp + i + 1, NMP)
        part = (br_src, gn_src)[o]
        return remote(part.at[to], m_recv.at[o, i], m_ss.at[o, i], m_rs.at[o, i], {"mp": to})

    for s in range(3):
        core_start(s)

    def fa_copy(s, q):
        return remote(fa_send.at[s, q], fa_recv.at[s, q], fa_ss.at[s, q], fa_rs.at[s, q], ahead)

    def ba_copy(s, q):
        return remote(ba_send.at[s, q], ba_recv.at[s, q], ba_ss.at[s, q], ba_rs.at[s, q], behind)

    def bx_copy(s, i):
        return remote(bx_send.at[s, i], bx_recv.at[s, i], bx_ss.at[s, i], bx_rs.at[s, i], x_peers[i])

    def fb_copy(s):
        return remote(fb_send.at[s], fb_recv.at[s], fb_ss.at[s], fb_rs.at[s], ahead)

    def bb_copy(s):
        return remote(bb_send.at[s], bb_recv.at[s], bb_ss.at[s], bb_rs.at[s], behind)

    def upper(d, q):
        return src[core, d, q, :HALF].astype(f32) + from_core[d, q, :HALF].astype(f32)

    def lower(d, q):
        return src[core, d, q, HALF:].astype(f32) + from_core[d, q, HALF:].astype(f32)

    def a_step(s, first=False, back=True):
        for q in range(NX):
            total = upper(f_dest(s), q)
            if not first:
                fa_copy(s - 1, q).wait_recv()
                total += fa_recv[s - 1, q].astype(f32)
            fa_send[s, q] = total.astype(bf16)
            fa_copy(s, q).start()
            if back:
                total = upper(b_dest(s), q)
                if not first:
                    ba_copy(s - 1, q).wait_recv()
                    total += ba_recv[s - 1, q].astype(f32)
                ba_send[s, q] = total.astype(bf16)
                ba_copy(s, q).start()

    def bx_step(s):
        core_copy(f_dest(s)).wait_recv()
        core_copy(b_dest(s)).wait_recv()
        for i in range(NX - 1):
            q = lax.rem(x + i + 1, NX)
            bx_send[s, i, 0] = lower(f_dest(s), q).astype(bf16)
            bx_send[s, i, 1] = lower(b_dest(s), q).astype(bf16)
            bx_copy(s, i).start()

    def row_sum(s, d, way):
        total = lower(d, x)
        for i in range(NX - 1):
            total += bx_recv[s, i, way].astype(f32)
        return total

    def bz_step(s, first=False, back=True):
        for i in range(NX - 1):
            bx_copy(s, i).wait_recv()
        total = row_sum(s, f_dest(s), 0)
        if not first:
            fb_copy(s - 1).wait_recv()
            total += fb_recv[s - 1].astype(f32)
        fb_send[s] = total.astype(bf16)
        fb_copy(s).start()
        if back:
            total = row_sum(s, b_dest(s), 1)
            if not first:
                bb_copy(s - 1).wait_recv()
                total += bb_recv[s - 1].astype(f32)
            bb_send[s] = total.astype(bf16)
            bb_copy(s).start()

    bx_step(0)
    a_step(0, first=True)
    core_start(3)
    bx_step(1)
    bz_step(0, first=True)
    a_step(1)
    core_start(4)
    bx_step(2)

    @pl.loop(2, BWD)
    def _(s):
        bz_step(s - 1)
        a_step(s)

        @pl.when(s < FWD - 3)
        def _():
            core_start(s + 3)

        bx_step(s + 1)

        @pl.when(s >= BWD - 3)
        def _():
            for o in range(2):
                m_copy(o, s - (BWD - 3)).start()

    bz_step(BWD - 1)
    a_step(FWD - 1, back=False)
    bz_step(FWD - 1, back=False)

    for q in range(NX):
        ba_copy(BWD - 1, q).wait_recv()
    for q in range(NX):
        fa_copy(FWD - 1, q).wait_recv()

    def whole(q):
        return (upper(z, q) + fa_recv[FWD - 1, q].astype(f32)
                + ba_recv[BWD - 1, q].astype(f32))

    x_copies = []
    for i, peer in enumerate(x_peers):
        x_send[i] = whole(lax.rem(x + i + 1, NX)).astype(bf16)
        copy = remote(x_send.at[i], x_recv.at[i], x_ss.at[i], x_rs.at[i], peer)
        copy.start()
        x_copies.append(copy)

    bb_copy(BWD - 1).wait_recv()
    fb_copy(FWD - 1).wait_recv()
    owned[HALF:] = (row_sum(FWD - 1, z, 1) + fb_recv[FWD - 1].astype(f32)
                    + bb_recv[BWD - 1].astype(f32))
    for o, (out, own_part) in enumerate(((br_out, br_src), (gn_out, gn_src))):
        total = own_part[mp].astype(f32)
        for i in range(NMP - 1):
            m_copy(o, i).wait_recv()
            total += m_recv[o, i].astype(f32)
        out[...] = total.astype(bf16)

    total = whole(x)
    for i in range(NX - 1):
        x_copies[i].wait_recv()
        total += x_recv[i].astype(f32)
    owned[:HALF] = total

    for copy in x_copies + [m_copy(o, i) for o in range(2) for i in range(NMP - 1)]:
        copy.wait_send()

    @pl.loop(0, NZ)
    def _(d):
        core_copy(d).wait_send()

    @pl.loop(0, FWD)
    def _(s):
        for q in range(NX):
            fa_copy(s, q).wait_send()
        for i in range(NX - 1):
            bx_copy(s, i).wait_send()
        fb_copy(s).wait_send()

    @pl.loop(0, BWD)
    def _(s):
        for q in range(NX):
            ba_copy(s, q).wait_send()
        bb_copy(s).wait_send()


def reduce_all(outgoing, branch_parts, gn_parts):
    vmem = pl.BlockSpec(memory_space=pltpu.VMEM)
    dma = pltpu.SemaphoreType.DMA
    part = (HALF, 2 * BLK)
    feats = jax.ShapeDtypeStruct((TOK, 256), bf16)

    def buf(*lead):
        return pltpu.VMEM(lead + part, bf16)

    return pl.pallas_call(
        reduce_kernel,
        out_shape=(jax.ShapeDtypeStruct((TOK, 128), f32), feats, feats),
        in_specs=[vmem, vmem, vmem],
        out_specs=(vmem, vmem, vmem),
        scratch_shapes=[
            pltpu.VMEM((NZ, NX, TOK, 128), bf16),
            buf(FWD, NX), buf(FWD, NX),
            buf(BWD, NX), buf(BWD, NX),
            buf(FWD, NX - 1, 2), buf(FWD, NX - 1, 2),
            buf(FWD), buf(FWD),
            buf(BWD), buf(BWD),
            buf(NX - 1), buf(NX - 1),
            pltpu.VMEM((2, NMP - 1, TOK, 256), bf16),
            dma((NZ,)), dma((NZ,)),
            dma((FWD, NX)), dma((FWD, NX)),
            dma((BWD, NX)), dma((BWD, NX)),
            dma((FWD, NX - 1)), dma((FWD, NX - 1)),
            dma((FWD,)), dma((FWD,)),
            dma((BWD,)), dma((BWD,)),
            dma((NX - 1,)), dma((NX - 1,)),
            dma((2, NMP - 1)), dma((2, NMP - 1)),
        ],
        compiler_params=pltpu.CompilerParams(
            collective_id=1, has_side_effects=True, vmem_limit_bytes=16 << 20),
        name="reduce_all",
    )(outgoing.reshape(2, NZ, NX, TOK, 128), branch_parts, gn_parts)


def body(x_in, gain, w_in, w_out, grad_out, block_cols, slots):
    whole_x, whole_grad, weights = gather_inputs(x_in, grad_out, w_in, w_out)
    outgoing, branch_parts, gn_parts = compute(
        block_cols, slots, whole_x, whole_grad, gain.reshape(NMP, 1, 256), weights)
    owned, branch, grad_normed = reduce_all(outgoing, branch_parts, gn_parts)
    owned = owned.reshape(4, BLK // 2, 2, BLK).transpose(0, 2, 1, 3).reshape(1, 4, BLK * BLK)
    return (branch, grad_normed, owned)


def solution(mesh):
    placed = (
        P("dp", "mp"),
        P(),
        P("mp", None),
        P("mp", None),
        P("dp", "mp"),
        P("mp", None),
        P("mp", None),
    )
    return jax.shard_map(
        body,
        mesh=mesh,
        in_specs=placed,
        out_specs=(P("dp", "mp"), P("dp", "mp"), P("mp", "dp", None)),
        check_vma=False,
    )
```

```python
import functools
import math

import jax
import jax.numpy as jnp
from jax import lax
from jax.experimental import pallas as pl
from jax.experimental.pallas import tpu as pltpu
from jax.sharding import PartitionSpec as P

BLK = 64
NRB = 16
KR = 16
NCB = 128
TOK = 128
NX = 4
NZ = 16
NMP = 4
FWD = NZ // 2
BWD = NZ - 1 - FWD
RELAY_AT = 8
HALF = 64

norm_eps = 1e-06
tanh_coef = 0.7978845608028654
f32 = jnp.float32
bf16 = jnp.bfloat16
MESH = pl.DeviceIdType.MESH
NT = (((1,), (1,)), ((), ()))
TN = (((0,), (0,)), ((), ()))


def signal_all(peers):
    barrier = pltpu.get_barrier_semaphore()
    for peer in peers:
        pl.semaphore_signal(barrier, inc=1, device_id=peer, device_id_type=MESH)
    pl.semaphore_wait(barrier, len(peers))


def remote(src, dst, send, recv, peer):
    return pltpu.make_async_remote_copy(
        src_ref=src, dst_ref=dst, send_sem=send, recv_sem=recv,
        device_id=peer, device_id_type=MESH,
    )


def gather_kernel(x_ref, g_ref, wi_hbm, wo_hbm, xo_ref, go_ref, w_ref,
                  wi, wo, s_in, s_out, send, recv, load):
    me = lax.axis_index("mp")
    loads = [pltpu.make_async_copy(wi_hbm, wi, load.at[0]),
             pltpu.make_async_copy(wo_hbm, wo, load.at[1]),
             pltpu.make_async_copy(x_ref, xo_ref.at[me], load.at[2]),
             pltpu.make_async_copy(g_ref, go_ref.at[me], load.at[3])]
    for copy in loads:
        copy.start()
    nxt, prv = lax.rem(me + 1, NMP), lax.rem(me + NMP - 1, NMP)
    ahead, behind = {"mp": nxt}, {"mp": prv}
    signal_all([ahead, behind])
    x_ahead = remote(x_ref, xo_ref.at[me], send.at[0], recv.at[0], ahead)
    g_behind = remote(g_ref, go_ref.at[me], send.at[1], recv.at[1], behind)
    g_ahead = remote(g_ref, go_ref.at[me], send.at[2], recv.at[2], ahead)
    x_behind = remote(x_ref, xo_ref.at[me], send.at[3], recv.at[3], behind)
    x_relay = remote(xo_ref.at[prv], xo_ref.at[prv], send.at[4], recv.at[4], ahead)
    g_relay = remote(go_ref.at[nxt], go_ref.at[nxt], send.at[5], recv.at[5], behind)
    for copy in (x_ahead, g_behind, g_ahead, x_behind):
        copy.start()
    for copy in loads:
        copy.wait()
    low = lax.broadcasted_iota(jnp.int32, (8, 2 * BLK), 1) < BLK
    square = (2 * BLK, 2 * BLK)
    eye = (lax.broadcasted_iota(jnp.int32, square, 0)
           == lax.broadcasted_iota(jnp.int32, square, 1)).astype(f32).astype(bf16)

    def relayout(r):
        top = pl.ds(pl.multiple_of(r * KR, KR), KR)
        for j in range(BLK // 2):
            lanes = slice(j * 2 * BLK, (j + 1) * 2 * BLK)
            v = wi[top, lanes].astype(f32)
            a, b = v[:8], v[8:]
            for par, u in enumerate((jnp.where(low, a, pltpu.roll(b, BLK, 1)),
                                     jnp.where(low, pltpu.roll(a, BLK, 1), b))):
                group, row = divmod(2 * j + par, 8)
                s_in[pl.ds(group * BLK + row, 8, stride=8), :] = u
            v = wo[top, lanes].astype(f32)
            for h in range(2):
                for par, u in enumerate((pltpu.roll(v[h * 8:h * 8 + 8], BLK, 1), v[h * 8:h * 8 + 8])):
                    group, row = divmod(2 * j + par, 8)
                    s_out[pl.ds((h * 8 + group) * BLK + row, 8, stride=8), :] = u
        for k in range(8):
            block = jnp.concatenate(
                [s_in[g * BLK + k * 8:g * BLK + k * 8 + 8, :] for g in range(8)], axis=0)
            turned = lax.dot_general(eye, block.astype(bf16), NT, preferred_element_type=f32)
            for h in range(2):
                kk = h * 8 + k
                lower = jnp.concatenate([
                    s_out[(h * 8 + g) * BLK + k * 8:(h * 8 + g) * BLK + k * 8 + 8, BLK:]
                    for g in range(8)], axis=0)
                both = jnp.concatenate([turned[h * BLK:(h + 1) * BLK], lower], axis=1)
                w_ref[pl.ds(pl.multiple_of((r * KR + kk) * BLK, BLK), BLK), :] = both.astype(bf16)

    pl.loop(0, RELAY_AT)(relayout)
    x_ahead.wait_recv()
    x_relay.start()
    g_behind.wait_recv()
    g_relay.start()
    pl.loop(RELAY_AT, NRB)(relayout)
    for copy in (g_ahead, x_behind, x_relay, g_relay):
        copy.wait_recv()
    for copy in (x_ahead, g_behind, g_ahead, x_behind, x_relay, g_relay):
        copy.wait_send()


def gather_inputs(x_in, grad_out, w_in, w_out):
    whole = jax.ShapeDtypeStruct((NMP, TOK, x_in.shape[1]), bf16)
    vmem = pl.BlockSpec(memory_space=pltpu.VMEM)
    hbm = pl.BlockSpec(memory_space=pltpu.HBM)
    return pl.pallas_call(
        gather_kernel,
        out_shape=(whole, whole, jax.ShapeDtypeStruct((NRB * KR * BLK, 2 * BLK), bf16)),
        in_specs=[hbm, hbm, hbm, hbm],
        out_specs=(vmem, vmem, vmem),
        scratch_shapes=[
            pltpu.VMEM(w_in.shape, bf16),
            pltpu.VMEM(w_out.shape, bf16),
            pltpu.VMEM((KR * BLK // 2, 2 * BLK), f32),
            pltpu.VMEM((KR * BLK, 2 * BLK), f32),
            pltpu.SemaphoreType.DMA((6,)),
            pltpu.SemaphoreType.DMA((6,)),
            pltpu.SemaphoreType.DMA((4,)),
        ],
        compiler_params=pltpu.CompilerParams(
            collective_id=0, has_side_effects=True, vmem_limit_bytes=16 << 20),
        name="gather_inputs",
    )(*(pltpu.with_memory_space_constraint(a, pltpu.HBM) for a in (x_in, grad_out, w_in, w_out)))


def compute_kernel(scale, cols, slots, x_ref, g_ref, gain_ref, w_ref,
                   out_ref, branch_ref, gn_ref,
                   normed, pre, gact, act, gpre, brt, gnt):
    squares = jnp.zeros((TOK, 1), f32)
    for p in range(NMP):
        xf = x_ref[p].astype(f32)
        squares += jnp.sum(xf * xf, axis=-1, keepdims=True)
    inv_rms = lax.rsqrt(squares / (NRB * BLK) + norm_eps)
    for p in range(NMP):
        normed[p] = (x_ref[p].astype(f32) * inv_rms * gain_ref[p]).astype(bf16)

    @pl.loop(0, NCB // 8)
    def _(i):
        rows = pl.ds(pl.multiple_of(i * (8 * BLK), 8 * BLK), 8 * BLK)
        pre[rows, :] = jnp.zeros((8 * BLK, TOK), f32)
        gact[rows, :] = jnp.zeros((8 * BLK, TOK), f32)

    blank = jnp.zeros((TOK, BLK), bf16)

    def stacked(top, bottom):
        return jnp.concatenate([
            jnp.concatenate([top, blank], axis=1),
            jnp.concatenate([blank, bottom], axis=1),
        ], axis=0)

    @pl.loop(0, NMP)
    def _(p):
        for q in range(NRB // NMP):
            r = p * (NRB // NMP) + q
            lanes = slice(q * BLK, (q + 1) * BLK)
            both = stacked(normed[p, :, lanes], g_ref[p, :, lanes])
            rows = pl.ds(pl.multiple_of(r * KR * BLK, KR * BLK), KR * BLK)
            parts = lax.dot_general(w_ref[rows, :], both, NT, preferred_element_type=f32)
            for k in range(KR):
                at = pl.ds(pl.multiple_of(cols[0, r * KR + k] * BLK, BLK), BLK)
                pre[at, :] += parts[k * BLK:(k + 1) * BLK, :TOK]
                gact[at, :] += parts[k * BLK:(k + 1) * BLK, TOK:]

    @pl.loop(0, NCB // 4)
    def _(i):
        rows = pl.ds(pl.multiple_of(i * (4 * BLK), 4 * BLK), 4 * BLK)
        v = pre[rows, :]
        square = v * v
        th = jnp.tanh(v * (tanh_coef + (tanh_coef * 0.044715) * square))
        rise = 0.5 + 0.5 * th
        value = v * rise
        act[rows, :] = value.astype(bf16)
        inner = tanh_coef + (tanh_coef * 0.134145) * square
        slope = rise + value * (1.0 - th) * inner
        gpre[rows, :] = (gact[rows, :] * slope).astype(bf16)
        for j in range(16):
            out_ref[i * 16 + j] = jnp.zeros((BLK // 2, 2 * BLK), bf16)

    @pl.loop(0, NMP)
    def _(p):
        for q in range(NRB // NMP):
            r = p * (NRB // NMP) + q
            lanes = slice(q * BLK, (q + 1) * BLK)
            n_r = normed[p, :, lanes]
            ats = [pl.ds(pl.multiple_of(cols[0, r * KR + k] * BLK, BLK), BLK) for k in range(KR)]
            gath = jnp.concatenate(
                [jnp.concatenate([gpre[at, :], act[at, :]], axis=1) for at in ats], axis=0)
            halves = jnp.concatenate([
                jnp.concatenate([gpre[at, :][:32], gpre[at, :][32:]], axis=1) for at in ats], axis=0)
            rows = pl.ds(pl.multiple_of(r * KR * BLK, KR * BLK), KR * BLK)
            sums = lax.dot_general(w_ref[rows, :], gath, TN, preferred_element_type=f32)
            at = pl.ds(pl.multiple_of(r * BLK, BLK), BLK)
            gnt[at, :] = sums[:BLK, :TOK]
            brt[at, :] = sums[BLK:, TOK:]
            grads = jnp.dot(halves, stacked(n_r, n_r), preferred_element_type=f32)
            grads = (grads * scale).astype(bf16)
            for k in range(KR):
                s = slots[0, r * KR + k]
                x, z, core, j = s // 128, (s // 8) % NZ, (s // 4) % 2, s % 4
                out_ref[((core * NZ + z) * NX + x) * 4 + j] = grads[k * 32:(k + 1) * 32]

    for p in range(NMP):
        rows = slice(p * 256, (p + 1) * 256)
        gn_ref[p] = gnt[rows, :].T.astype(bf16)
        branch_ref[p] = brt[rows, :].T.astype(bf16)


def compute(cols, slots, whole_x, whole_grad, gain, weights):
    vmem = pl.BlockSpec(memory_space=pltpu.VMEM)
    smem = pl.BlockSpec(memory_space=pltpu.SMEM)
    feats = jax.ShapeDtypeStruct((NMP, TOK, 256), bf16)
    scale = 1.0 / math.sqrt(TOK * 2 * NX * NZ)
    return pl.pallas_call(
        functools.partial(compute_kernel, scale),
        out_shape=(jax.ShapeDtypeStruct((512, BLK // 2, 2 * BLK), bf16), feats, feats),
        in_specs=[smem, smem, vmem, vmem, vmem, vmem],
        out_specs=(vmem, vmem, vmem),
        scratch_shapes=[
            pltpu.VMEM((NMP, TOK, 256), bf16),
            pltpu.VMEM((NCB * BLK, TOK), f32),
            pltpu.VMEM((NCB * BLK, TOK), f32),
            pltpu.VMEM((NCB * BLK, TOK), bf16),
            pltpu.VMEM((NCB * BLK, TOK), bf16),
            pltpu.VMEM((NRB * BLK, TOK), f32),
            pltpu.VMEM((NRB * BLK, TOK), f32),
        ],
        compiler_params=pltpu.CompilerParams(vmem_limit_bytes=24 << 20),
        name="local_compute",
    )(cols, slots, whole_x, whole_grad, gain, weights)


def reduce_kernel(src, br_src, gn_src, owned, br_out, gn_out,
                  from_core, fa_send, fa_recv, ba_send, ba_recv, bx_send, bx_recv,
                  fb_send, fb_recv, bb_send, bb_recv, x_send, x_recv, m_recv,
                  core_ss, core_rs, fa_ss, fa_rs, ba_ss, ba_rs, bx_ss, bx_rs,
                  fb_ss, fb_rs, bb_ss, bb_rs, x_ss, x_rs, m_ss, m_rs):
    dp, mp = lax.axis_index("dp"), lax.axis_index("mp")
    core = lax.rem(dp, 2)
    z = lax.rem(dp // 2, NZ)
    x = dp // (2 * NZ)

    def at(xx, zz, cc):
        return {"dp": (xx * NZ + zz) * 2 + cc}

    partner = at(x, z, 1 - core)
    ahead = at(x, lax.rem(z + 1, NZ), core)
    behind = at(x, lax.rem(z + NZ - 1, NZ), core)
    x_peers = [at(lax.rem(x + i, NX), z, core) for i in range(1, NX)]
    m_peers = [{"mp": lax.rem(mp + i, NMP)} for i in range(1, NMP)]
    signal_all([partner, ahead, behind] + x_peers + m_peers)

    def f_dest(s):
        return lax.rem(z + FWD - s, NZ)

    def b_dest(s):
        return lax.rem(z + NZ - BWD + s, NZ)

    def core_copy(d):
        return remote(src.at[1 - core, d], from_core.at[d], core_ss.at[d], core_rs.at[d], partner)

    def core_start(s):
        core_copy(f_dest(s)).start()
        core_copy(b_dest(s)).start()

    def m_copy(o, i):
        to = lax.rem(mp + i + 1, NMP)
        part = (br_src, gn_src)[o]
        return remote(part.at[to], m_recv.at[o, i], m_ss.at[o, i], m_rs.at[o, i], {"mp": to})

    for s in range(3):
        core_start(s)

    def fa_copy(s, q):
        return remote(fa_send.at[s, q], fa_recv.at[s, q], fa_ss.at[s, q], fa_rs.at[s, q], ahead)

    def ba_copy(s, q):
        return remote(ba_send.at[s, q], ba_recv.at[s, q], ba_ss.at[s, q], ba_rs.at[s, q], behind)

    def bx_copy(s, i):
        return remote(bx_send.at[s, i], bx_recv.at[s, i], bx_ss.at[s, i], bx_rs.at[s, i], x_peers[i])

    def fb_copy(s):
        return remote(fb_send.at[s], fb_recv.at[s], fb_ss.at[s], fb_rs.at[s], ahead)

    def bb_copy(s):
        return remote(bb_send.at[s], bb_recv.at[s], bb_ss.at[s], bb_rs.at[s], behind)

    def upper(d, q):
        return src[core, d, q, :HALF].astype(f32) + from_core[d, q, :HALF].astype(f32)

    def lower(d, q):
        return src[core, d, q, HALF:].astype(f32) + from_core[d, q, HALF:].astype(f32)

    def a_step(s, first=False, back=True):
        for q in range(NX):
            total = upper(f_dest(s), q)
            if not first:
                fa_copy(s - 1, q).wait_recv()
                total += fa_recv[s - 1, q].astype(f32)
            fa_send[s, q] = total.astype(bf16)
            fa_copy(s, q).start()
            if back:
                total = upper(b_dest(s), q)
                if not first:
                    ba_copy(s - 1, q).wait_recv()
                    total += ba_recv[s - 1, q].astype(f32)
                ba_send[s, q] = total.astype(bf16)
                ba_copy(s, q).start()

    def bx_step(s):
        core_copy(f_dest(s)).wait_recv()
        core_copy(b_dest(s)).wait_recv()
        for i in range(NX - 1):
            q = lax.rem(x + i + 1, NX)
            bx_send[s, i, 0] = lower(f_dest(s), q).astype(bf16)
            bx_send[s, i, 1] = lower(b_dest(s), q).astype(bf16)
            bx_copy(s, i).start()

    def row_sum(s, d, way):
        total = lower(d, x)
        for i in range(NX - 1):
            total += bx_recv[s, i, way].astype(f32)
        return total

    def bz_step(s, first=False, back=True):
        for i in range(NX - 1):
            bx_copy(s, i).wait_recv()
        total = row_sum(s, f_dest(s), 0)
        if not first:
            fb_copy(s - 1).wait_recv()
            total += fb_recv[s - 1].astype(f32)
        fb_send[s] = total.astype(bf16)
        fb_copy(s).start()
        if back:
            total = row_sum(s, b_dest(s), 1)
            if not first:
                bb_copy(s - 1).wait_recv()
                total += bb_recv[s - 1].astype(f32)
            bb_send[s] = total.astype(bf16)
            bb_copy(s).start()

    bx_step(0)
    a_step(0, first=True)
    core_start(3)
    bx_step(1)
    bz_step(0, first=True)
    a_step(1)
    core_start(4)
    bx_step(2)

    @pl.loop(2, BWD)
    def _(s):
        bz_step(s - 1)
        a_step(s)

        @pl.when(s < FWD - 3)
        def _():
            core_start(s + 3)

        bx_step(s + 1)

        @pl.when(s >= BWD - 3)
        def _():
            for o in range(2):
                m_copy(o, s - (BWD - 3)).start()

    bz_step(BWD - 1)
    a_step(FWD - 1, back=False)
    bz_step(FWD - 1, back=False)

    for q in range(NX):
        ba_copy(BWD - 1, q).wait_recv()
    for q in range(NX):
        fa_copy(FWD - 1, q).wait_recv()

    def whole(q):
        return (upper(z, q) + fa_recv[FWD - 1, q].astype(f32)
                + ba_recv[BWD - 1, q].astype(f32))

    x_copies = []
    for i, peer in enumerate(x_peers):
        x_send[i] = whole(lax.rem(x + i + 1, NX)).astype(bf16)
        copy = remote(x_send.at[i], x_recv.at[i], x_ss.at[i], x_rs.at[i], peer)
        copy.start()
        x_copies.append(copy)

    bb_copy(BWD - 1).wait_recv()
    fb_copy(FWD - 1).wait_recv()
    owned[HALF:] = (row_sum(FWD - 1, z, 1) + fb_recv[FWD - 1].astype(f32)
                    + bb_recv[BWD - 1].astype(f32))
    for o, (out, own_part) in enumerate(((br_out, br_src), (gn_out, gn_src))):
        total = own_part[mp].astype(f32)
        for i in range(NMP - 1):
            m_copy(o, i).wait_recv()
            total += m_recv[o, i].astype(f32)
        out[...] = total.astype(bf16)

    total = whole(x)
    for i in range(NX - 1):
        x_copies[i].wait_recv()
        total += x_recv[i].astype(f32)
    owned[:HALF] = total

    for copy in x_copies + [m_copy(o, i) for o in range(2) for i in range(NMP - 1)]:
        copy.wait_send()

    @pl.loop(0, NZ)
    def _(d):
        core_copy(d).wait_send()

    @pl.loop(0, FWD)
    def _(s):
        for q in range(NX):
            fa_copy(s, q).wait_send()
        for i in range(NX - 1):
            bx_copy(s, i).wait_send()
        fb_copy(s).wait_send()

    @pl.loop(0, BWD)
    def _(s):
        for q in range(NX):
            ba_copy(s, q).wait_send()
        bb_copy(s).wait_send()


def reduce_all(outgoing, branch_parts, gn_parts):
    vmem = pl.BlockSpec(memory_space=pltpu.VMEM)
    dma = pltpu.SemaphoreType.DMA
    part = (HALF, 2 * BLK)
    feats = jax.ShapeDtypeStruct((TOK, 256), bf16)

    def buf(*lead):
        return pltpu.VMEM(lead + part, bf16)

    return pl.pallas_call(
        reduce_kernel,
        out_shape=(jax.ShapeDtypeStruct((TOK, 128), f32), feats, feats),
        in_specs=[vmem, vmem, vmem],
        out_specs=(vmem, vmem, vmem),
        scratch_shapes=[
            pltpu.VMEM((NZ, NX, TOK, 128), bf16),
            buf(FWD, NX), buf(FWD, NX),
            buf(BWD, NX), buf(BWD, NX),
            buf(FWD, NX - 1, 2), buf(FWD, NX - 1, 2),
            buf(FWD), buf(FWD),
            buf(BWD), buf(BWD),
            buf(NX - 1), buf(NX - 1),
            pltpu.VMEM((2, NMP - 1, TOK, 256), bf16),
            dma((NZ,)), dma((NZ,)),
            dma((FWD, NX)), dma((FWD, NX)),
            dma((BWD, NX)), dma((BWD, NX)),
            dma((FWD, NX - 1)), dma((FWD, NX - 1)),
            dma((FWD,)), dma((FWD,)),
            dma((BWD,)), dma((BWD,)),
            dma((NX - 1,)), dma((NX - 1,)),
            dma((2, NMP - 1)), dma((2, NMP - 1)),
        ],
        compiler_params=pltpu.CompilerParams(
            collective_id=1, has_side_effects=True, vmem_limit_bytes=16 << 20),
        name="reduce_all",
    )(outgoing.reshape(2, NZ, NX, TOK, 128), branch_parts, gn_parts)


def body(x_in, gain, w_in, w_out, grad_out, block_cols, slots):
    whole_x, whole_grad, weights = gather_inputs(x_in, grad_out, w_in, w_out)
    outgoing, branch_parts, gn_parts = compute(
        block_cols, slots, whole_x, whole_grad, gain.reshape(NMP, 1, 256), weights)
    owned, branch, grad_normed = reduce_all(outgoing, branch_parts, gn_parts)
    owned = owned.reshape(4, BLK // 2, 2, BLK).transpose(0, 2, 1, 3).reshape(1, 4, BLK * BLK)
    return (branch, grad_normed, owned)


def solution(mesh):
    placed = (
        P("dp", "mp"),
        P(),
        P("mp", None),
        P("mp", None),
        P("dp", "mp"),
        P("mp", None),
        P("mp", None),
    )
    return jax.shard_map(
        body,
        mesh=mesh,
        in_specs=placed,
        out_specs=(P("dp", "mp"), P("dp", "mp"), P("mp", "dp", None)),
        check_vma=False,
    )
```
